32 devices in a mesh: pole: 2 (over x), row: 8 (over z, y), col: 2 (over core).
Axes of the slice: x: 2, y: 2, z: 4, core: 2. Of those that a mesh axis runs over, the one named last changes fastest.
Arguments:
- ancestor_inverse: float32 [2, 24576, 12288], P(None, ('pole', 'row'), 'col'), parts along dimension 1, may hold values from -6 to 6
- factor_panels: float32 [4, 2, 24576, 128], P(None, None, ('pole', 'col', 'row')), parts along dimension 2, may hold values from -0.0546875 to 0.0546875
- diag_inverse: float32 [8, 2, 128, 128], P('pole'), parts along dimension 0, may hold values from -6 to 6
- coupling: float32 [4, 2, 128, 128], P('pole'), parts along dimension 0, may hold values from -0.5 to 0.5
- block_pattern: int32 [4, 96], replicated, may hold values from 0 to 1, as said below
- tree_order: int32 [4], replicated, may hold values from 0 to 3, each once
Outputs:
- inverse_panels: float32 [4, 2, 24576, 128], P(None, None, ('pole', 'row')), parts along dimension 2
- inverse_diagonal: float32 [8, 2, 128, 128], P('pole'), parts along dimension 0
- inverse_coupling: float32 [4, 2, 128, 128], P('pole'), parts along dimension 0
The draws below stay inside these ranges and needn't reach their ends.
There are 2 independent parts, one for each index of `pole`. The reference program is written for one: setup_inputs(seed, part) draws one part's arguments, and reference() takes and returns one part's arrays. A program takes and returns all parts, laid end to end along the dimension named above; an argument that names none is the same for every part. Nothing has to cross between parts.
Inputs may be any that keep to these rules, and one draw needn't show every extreme that they name: `tree_order`: each supernode number appears once. `block_pattern`: blocks 0 and 48 lie in every supernode's structure.
All inputs are finite; a program needn't handle non-finite values.
Results may differ from the reference program's by a relative error of at most 0.0001.
Values sent between devices are 32-bit elements; how exact they have to be, the bound alone decides.
A program may use at most 192 MiB of HBM per device.

```python
import jax
import jax.numpy as jnp
from jax import lax

B = 128
ANC = 12288
SUPER = 4
NB = 96


def draw_block_pattern(key, part):
    random_level = jax.random.randint(key, (SUPER, NB), 0, 8)
    pattern_live = (random_level < 5).astype(jnp.int32)
    block_index = jnp.arange(NB, dtype=jnp.int32)
    forced_blocks = ((block_index == 0) | (block_index == NB // 2)).astype(jnp.int32)
    return jnp.maximum(pattern_live, forced_blocks[None, :])


def block_levels(rng, extent, cuts, least, high):
    loudness, own = 1.0, jax.random.fold_in(rng, 6)
    for axis_at, shards_of in cuts:
        draws = jnp.exp(jax.random.uniform(jax.random.fold_in(own, axis_at), (shards_of,), jnp.float32, least / len(cuts), high / len(cuts)))
        loudness = loudness * jnp.repeat(draws, extent[axis_at] // shards_of).reshape([-1 if axis == axis_at else 1 for axis in range(len(extent))])
    return loudness


def normal_values(key, shape, width, reach, shards=(), kind=jnp.bfloat16):
    gain = block_levels(key, shape, shards, -0.22, 0.18) if shards else 1.0
    array = jax.random.normal(key, shape, jnp.float32) * width * gain
    return jnp.minimum(jnp.maximum(array, -reach), reach).astype(kind)


def setup_inputs(seed: int = 0, part: int = 0) -> dict:
    splits = jax.random.split(jax.random.key(seed), 7)
    part_splits = jax.random.split(jax.random.fold_in(splits[6], part), 7)
    ancestor_inverse = normal_values(part_splits[0], (2, ANC, ANC), 1.0, 6.0, ((1, 8), (2, 2)), jnp.float32)
    factor_panels = normal_values(part_splits[1], (SUPER, 2, ANC, B), ANC ** -0.5, 0.0546875, ((2, 16),), jnp.float32)
    diag_inverse = normal_values(part_splits[2], (SUPER, 2, B, B), 1.0, 6.0, (), jnp.float32)
    coupling = normal_values(part_splits[3], (SUPER // 2, 2, B, B), B ** -0.5, 0.5, (), jnp.float32)
    block_pattern = draw_block_pattern(jax.random.fold_in(splits[6], 71), part)
    tree_order = jax.random.permutation(splits[5], SUPER).astype(jnp.int32)
    return {"ancestor_inverse": ancestor_inverse, "factor_panels": factor_panels, "diag_inverse": diag_inverse, "coupling": coupling, "block_pattern": block_pattern, "tree_order": tree_order}


def matmul(left_side, right_side):
    return jnp.dot(left_side, right_side, preferred_element_type=jnp.float32, precision=lax.Precision.HIGHEST)


def multiply(left_side, right_side):
    real_part = matmul(left_side[0], right_side[0]) - matmul(left_side[1], right_side[1])
    imag_part = matmul(left_side[0], right_side[1]) + matmul(left_side[1], right_side[0])
    return jnp.stack([real_part, imag_part])


def flipped(matrix):
    return jnp.swapaxes(matrix, 1, 2)


def reference(ancestor_inverse, factor_panels, diag_inverse, coupling, block_pattern, tree_order):
    row_masks = jnp.repeat(block_pattern.astype(jnp.float32), B, axis=1)
    sorted_masks = jnp.take(row_masks, tree_order, axis=0)
    masks = jnp.concatenate([sorted_masks[:2], sorted_masks[2:] * sorted_masks[:2]], axis=0)
    panels = jnp.take(factor_panels, tree_order, axis=0) * masks[:, None, :, None]
    diag_blocks = jnp.take(diag_inverse, tree_order, axis=0)
    parent_cols = []
    parent_diag = []
    for tree_slot in range(2):
        column_block = -masks[tree_slot][None, :, None] * multiply(ancestor_inverse, panels[tree_slot])
        parent_cols.append(column_block)
        parent_diag.append(diag_blocks[tree_slot] - multiply(flipped(panels[tree_slot]), column_block))
    child_cols = []
    child_diag = []
    crosses = []
    for tree_slot in range(2):
        child_slot = tree_slot + 2
        link_block = coupling[tree_slot]
        column_block = -masks[child_slot][None, :, None] * (
            multiply(ancestor_inverse, panels[child_slot]) + multiply(parent_cols[tree_slot], link_block))
        cross_block = -(multiply(flipped(parent_cols[tree_slot]), panels[child_slot])
                        + multiply(parent_diag[tree_slot], link_block))
        child_cols.append(column_block)
        crosses.append(cross_block)
        child_diag.append(diag_blocks[child_slot] - multiply(flipped(panels[child_slot]), column_block)
                          - multiply(flipped(link_block), cross_block))
    all_cols = jnp.stack(parent_cols + child_cols)
    all_diag = jnp.stack(parent_diag + child_diag)
    inverse_panels = jnp.zeros_like(factor_panels).at[tree_order].set(all_cols)
    inverse_diagonal = jnp.zeros_like(diag_inverse).at[tree_order].set(all_diag)
    return inverse_panels, inverse_diagonal, jnp.stack(crosses)
```

```python
import functools
import math

import jax
import jax.numpy as jnp
from jax import lax
from jax.experimental import pallas as pl
from jax.experimental.pallas import tpu as pltpu
from jax.sharding import PartitionSpec as P

BF16 = jnp.bfloat16
F32 = jnp.float32
GROUP = 8
VMEM_BYTES = 64 * 1024 * 1024 - 256 * 1024


def swapped(block, axis, bit):
    count = lax.axis_size(axis)
    route = []
    for low in range(count):
        high = low | 1 << bit
        if high != low and high < count:
            route += [(low, high), (high, low)]
    return lax.ppermute(block, axis, route)


def matmul(left_side, right_side):
    return jnp.dot(
        left_side, right_side, preferred_element_type=jnp.float32, precision=lax.Precision.HIGHEST
    )


def multiply(left_side, right_side):
    real_part = matmul(left_side[0], right_side[0]) - matmul(left_side[1], right_side[1])
    imag_part = matmul(left_side[0], right_side[1]) + matmul(left_side[1], right_side[0])
    return jnp.stack([real_part, imag_part])


def flipped(matrix):
    return jnp.swapaxes(matrix, 1, 2)


def row_masks(pattern_eff, first_row, row_count, block_rows):
    row_index = first_row + jnp.arange(row_count, dtype=jnp.int32)
    blocks = row_index // block_rows
    onehot = (blocks[:, None] == jnp.arange(pattern_eff.shape[1], dtype=jnp.int32)[None, :]).astype(
        jnp.float32
    )
    return matmul(pattern_eff, onehot.T)


def per_device_dense(ancestor_inverse, factor_panels, diag_inverse, coupling, block_pattern, tree_order):
    grid_row = lax.axis_index("row")
    grid_col = lax.axis_index("col")
    tile_rows = ancestor_inverse.shape[1]
    half_rows = ancestor_inverse.shape[2]
    piece_rows = factor_panels.shape[2]
    block_rows = factor_panels.shape[3]
    super_count = factor_panels.shape[0]
    share_rows = tile_rows // 2
    sorted_pattern = jnp.take(block_pattern, tree_order, axis=0).astype(jnp.float32)
    pattern_eff = jnp.concatenate(
        [sorted_pattern[:2], sorted_pattern[2:] * sorted_pattern[:2]], axis=0
    )
    source_mask = row_masks(
        pattern_eff, grid_col * half_rows + grid_row * piece_rows, piece_rows, block_rows
    )
    target_mask = row_masks(pattern_eff, grid_row * tile_rows, tile_rows, block_rows)
    panels = jnp.take(factor_panels, tree_order, axis=0) * source_mask[:, None, :, None]
    diag_blocks = jnp.take(diag_inverse, tree_order, axis=0)
    columns = []
    products = []
    for tree_slot in range(super_count):
        gathered = lax.all_gather(panels[tree_slot], "row", axis=1, tiled=True)
        columns.append(gathered)
        products.append(lax.psum(multiply(ancestor_inverse, gathered), "col"))
    own_flag = (grid_row * tile_rows // half_rows == grid_col).astype(jnp.float32)
    offset = jnp.clip(grid_row * tile_rows - grid_col * half_rows, 0, half_rows - tile_rows)
    own_windows = jnp.stack(
        [
            lax.dynamic_slice_in_dim(column_set, offset, tile_rows, 1) * own_flag
            for column_set in columns
        ]
    )
    partner_windows = swapped(own_windows, "col", 0)
    tile_windows = own_windows + partner_windows

    def share(matrix):
        return lax.dynamic_slice_in_dim(matrix, grid_col * share_rows, share_rows, 1)

    windows = [share(tile_windows[tree_slot]) for tree_slot in range(super_count)]
    parent_cols = [
        -target_mask[tree_slot][None, :, None] * products[tree_slot] for tree_slot in range(2)
    ]
    child_cols = [
        -target_mask[tree_slot + 2][None, :, None]
        * (products[tree_slot + 2] + multiply(parent_cols[tree_slot], coupling[tree_slot]))
        for tree_slot in range(2)
    ]
    parent_local = [
        multiply(flipped(windows[tree_slot]), share(parent_cols[tree_slot]))
        for tree_slot in range(2)
    ]
    cross_local = [
        multiply(flipped(share(parent_cols[tree_slot])), windows[tree_slot + 2])
        for tree_slot in range(2)
    ]
    child_local = [
        multiply(flipped(windows[tree_slot + 2]), share(child_cols[tree_slot]))
        for tree_slot in range(2)
    ]
    parent_sums = lax.psum(jnp.stack(parent_local), ("row", "col"))
    parent_diag = [diag_blocks[tree_slot] - parent_sums[tree_slot] for tree_slot in range(2)]
    child_totals = lax.psum(jnp.stack(cross_local + child_local), ("row", "col"))
    crosses = [
        -(child_totals[tree_slot] + multiply(parent_diag[tree_slot], coupling[tree_slot]))
        for tree_slot in range(2)
    ]
    child_sums = [child_totals[2 + tree_slot] for tree_slot in range(2)]
    child_diag = [
        diag_blocks[tree_slot + 2]
        - child_sums[tree_slot]
        - multiply(flipped(coupling[tree_slot]), crosses[tree_slot])
        for tree_slot in range(2)
    ]
    all_cols = jnp.stack(parent_cols + child_cols)
    all_diag = jnp.stack(parent_diag + child_diag)
    inverse_panels = jnp.zeros_like(all_cols).at[tree_order].set(all_cols)
    inverse_diagonal = jnp.zeros_like(all_diag).at[tree_order].set(all_diag)
    return (inverse_panels, inverse_diagonal, jnp.stack(crosses))


def halves(value):
    high = value.astype(BF16)
    return high, (value - high.astype(F32)).astype(BF16)


def pack_kernel(source_ref, *refs):
    *panel_refs, packed_ref = refs
    for at, panel_ref in enumerate(panel_refs):
        packed_ref[at] = panel_ref[0].reshape(packed_ref.shape[1:])


def pack(factor_panels, supernode, block, size):
    count = block.shape[0]
    together = math.gcd(count, 4)

    def panel_map(at, g, source):
        return (source[0, g * together + at], 0, source[1, g * together + at], 0)

    return pl.pallas_call(
        pack_kernel,
        out_shape=jax.ShapeDtypeStruct((count, 2 * size, size), F32),
        grid_spec=pltpu.PrefetchScalarGridSpec(
            num_scalar_prefetch=1,
            grid=(count // together,),
            in_specs=[
                pl.BlockSpec((1, 2, size, size), functools.partial(panel_map, at))
                for at in range(together)
            ],
            out_specs=pl.BlockSpec((together, 2 * size, size), lambda g, source: (g, 0, 0)),
        ),
    )(jnp.stack([supernode, block]), *[factor_panels] * together)


ROW_CHUNK = 256


def relay_plan(lines, count, block_us, unit_us, units):
    first = max(1, round(count / 6))
    rest = count - first
    cuts = [first + rest * at // 3 for at in range(4)]
    parts = [(0, first)] + [(cuts[at], cuts[at + 1]) for at in range(3)]
    cost = [(high - low) * block_us for low, high in parts]
    beside_time = cost[0]

    def stream(own_items, forwarded):
        clock, landed = 0.0, {}
        for item, ready in own_items + forwarded:
            clock = max(clock, ready) + cost[item[2]]
            landed[item] = clock
        return landed

    climbs = {}
    for way in (1, -1):
        order = range(lines) if way == 1 else range(lines - 1, -1, -1)
        before = {}
        for z in order:
            climbs[way, z] = before
            own = [((z, 0, part), 0.0) for part in (1, 2, 3, 0)] + [((z, 1, 0), beside_time)]
            before = stream(own, sorted(before.items(), key=lambda pair: pair[1]))
    plans = []
    for z in range(lines):
        landed = {**climbs[1, z], **climbs[-1, z]}
        crossing = sorted(
            ((item, when) for item, when in landed.items() if item[1] == 0 and item[2] > 0),
            key=lambda pair: pair[1],
        )
        across = stream([((z, 0, part), 0.0) for part in (0, 1, 2, 3)], crossing)
        ready = {(z, 0): 0.0}
        for item, when in landed.items():
            key = item[:2]
            ready[key] = max(ready.get(key, 0.0), when)
        for item, when in across.items():
            key = (item[0], 1)
            ready[key] = max(ready.get(key, 0.0), when)
        events = sorted([((z, 1, 0), beside_time)] + list(landed.items()), key=lambda pair: pair[1])
        pieces = sorted(ready, key=lambda key: ready[key])
        clock, at, before_unit, after = 0.0, 0, {}, []
        for turn, piece in enumerate(pieces):
            for unit in range(units):
                start = max(clock, ready[piece]) if unit == 0 else clock
                while at < len(events) and events[at][1] <= start:
                    before_unit.setdefault(turn * units + unit, []).append(events[at][0])
                    at += 1
                clock = start + unit_us
        after = [event for event, _ in events[at:]]
        plans.append((pieces, before_unit, after))
    return parts, plans


def gather_product_kernel(
    rows, parts, plans, size,
    place_ref, own_ref, a_ref, all_ref, mine_ref, other_ref,
    staged, a_stage, b_high, b_low, acc, mine,
    send_sem, recv_sem, load_sem, keep_sem, a_sem, mine_sem, swap_send, swap_recv,
):
    here = lax.axis_index("row")
    sibling = 1 - lax.axis_index("col")
    lines = rows // 2
    z, y = here // 2, here % 2
    count = parts[-1][1]
    chunk_rows = a_stage.shape[2]
    chunks = a_ref.shape[1] // chunk_rows
    width = b_high.shape[1]
    blocks = width // size
    beside = z * 2 + (1 - y)
    up, down = here + 2, here - 2
    has_up, has_down = z < lines - 1, z > 0

    def copy(part, origin, way, target, own=False):
        low, high = parts[part]
        span = pl.ds(low, high - low)
        return pltpu.make_async_remote_copy(
            src_ref=own_ref.at[span] if own else all_ref.at[origin, span],
            dst_ref=all_ref.at[origin, span],
            send_sem=send_sem.at[part, origin, way],
            recv_sem=recv_sem.at[part, origin],
            device_id={"row": target},
            device_id_type=pl.DeviceIdType.MESH,
        )

    def arrived(part, origin):
        copy(part, origin, 0, beside).wait_recv()

    barrier = pltpu.get_barrier_semaphore()

    def greet(target):
        pl.semaphore_signal(barrier, inc=1, device_id=target, device_id_type=pl.DeviceIdType.MESH)

    greet({"row": beside})
    greet({"col": sibling})

    @pl.when(has_up)
    def _():
        greet({"row": up})

    @pl.when(has_down)
    def _():
        greet({"row": down})

    pl.semaphore_wait(barrier, 2 + has_up.astype(jnp.int32) + has_down.astype(jnp.int32))

    copy(0, here, 2, beside, True).start()
    for part in (1, 2, 3, 0):
        @pl.when(has_up)
        def _():
            copy(part, here, 0, up, True).start()

        @pl.when(has_down)
        def _():
            copy(part, here, 1, down, True).start()

        if part:
            copy(part, here, 2, beside, True).start()

    def origin_of(turn):
        origin = here
        for line, (pieces, _, _) in enumerate(plans):
            for at, (from_line, side) in enumerate(pieces):
                origin = jnp.where(
                    (z == line) & (turn == at), from_line * 2 + (y if side == 0 else 1 - y), origin
                )
        return origin

    def a_copy(step, origin):
        chunk = step % chunks
        return pltpu.make_async_copy(
            a_ref.at[
                :,
                pl.ds(pl.multiple_of(chunk * chunk_rows, 8), chunk_rows),
                pl.ds(pl.multiple_of(origin * width, 128), width),
            ],
            a_stage.at[step % 2],
            a_sem.at[step % 2],
        )

    a_copy(0, origin_of(0)).start()
    a_copy(1, origin_of(1 // chunks)).start()
    acc[...] = jnp.zeros_like(acc)
    staged[0] = jnp.zeros(staged.shape[1:], F32)

    def relay(line, item):
        from_line, side, part = item
        origin = from_line * 2 + (y if side == 0 else 1 - y)
        arrived(part, origin)
        if from_line == line:
            ways = ([0] if line < lines - 1 else []) + ([1] if line > 0 else [])
        elif from_line < line:
            ways = [0] if line < lines - 1 else []
        else:
            ways = [1] if line > 0 else []
        for way in ways:
            copy(part, origin, way, up if way == 0 else down).start()
        if side == 0 and part:
            copy(part, origin, 2, beside).start()

    def a_step(step, _):
        turn, chunk = step // chunks, step % chunks
        for line, (pieces, before_unit, _) in enumerate(plans):
            @pl.when(z == line)
            def _():
                for at in sorted(before_unit):
                    @pl.when(step == at)
                    def _():
                        for item in before_unit[at]:
                            relay(line, item)

        @pl.when(chunk == 0)
        def _():
            for line, (pieces, _, _) in enumerate(plans):
                for at, (from_line, side) in enumerate(pieces):
                    if side == 1:
                        @pl.when((z == line) & (turn == at))
                        def _():
                            for part in (1, 2, 3):
                                arrived(part, from_line * 2 + (1 - y))

            origin = origin_of(turn)

            @pl.when(turn == 0)
            def _():
                load = pltpu.make_async_copy(own_ref.at[pl.ds(0, count)], staged.at[pl.ds(1, count)], load_sem)
                load.start()
                load.wait()
                pltpu.make_async_copy(
                    staged.at[pl.ds(1, count)], all_ref.at[here, pl.ds(0, count)], keep_sem
                ).start()

            @pl.when(turn == 1)
            def _():
                pltpu.make_async_copy(
                    staged.at[pl.ds(1, count)], all_ref.at[here, pl.ds(0, count)], keep_sem
                ).wait()

            @pl.when(turn > 0)
            def _():
                load = pltpu.make_async_copy(
                    all_ref.at[origin, pl.ds(0, count)], staged.at[pl.ds(1, count)], load_sem
                )
                load.start()
                load.wait()

            def spread(block, _):
                span = pl.ds(pl.multiple_of(block * size, size), size)
                for slot in range(4):
                    value = staged[place_ref[origin * (4 * blocks) + slot * blocks + block]]
                    real, imag = value[:size], value[size:]
                    for kind, term in enumerate((real, imag, real + imag)):
                        high, low = halves(term)
                        b_high[kind, span, slot * size:(slot + 1) * size] = high
                        b_low[kind, span, slot * size:(slot + 1) * size] = low
                return 0

            lax.fori_loop(0, blocks, spread, 0)

        a_copy(step, here).wait()
        span = pl.ds(pl.multiple_of(chunk * chunk_rows, 8), chunk_rows)
        real, imag = a_stage[step % 2, 0], a_stage[step % 2, 1]
        for kind, term in enumerate((real, imag, real + imag)):
            high, low = halves(term)
            acc[kind, span, :] += jnp.dot(
                jnp.concatenate([high, low, high], axis=1),
                jnp.concatenate([b_high[kind], b_high[kind], b_low[kind]], axis=0),
                preferred_element_type=F32,
            )

        @pl.when(step + 2 < rows * chunks)
        def _():
            a_copy(step + 2, origin_of((step + 2) // chunks)).start()

        @pl.when(turn == rows - 1)
        def _():
            for slot in range(4):
                columns = slice(slot * size, (slot + 1) * size)
                first, second = acc[0, span, columns], acc[1, span, columns]
                mine[slot, 0, span] = first - second
                mine[slot, 1, span] = acc[2, span, columns] - first - second
            swap(chunk).start()
            keep_mine(chunk).start()

        return 0

    def swap(chunk):
        span = pl.ds(pl.multiple_of(chunk * chunk_rows, 8), chunk_rows)
        return pltpu.make_async_remote_copy(
            src_ref=mine.at[:, :, span],
            dst_ref=other_ref.at[:, :, span],
            send_sem=swap_send.at[chunk],
            recv_sem=swap_recv.at[chunk],
            device_id={"col": sibling},
            device_id_type=pl.DeviceIdType.MESH,
        )

    def keep_mine(chunk):
        span = pl.ds(pl.multiple_of(chunk * chunk_rows, 8), chunk_rows)
        return pltpu.make_async_copy(mine.at[:, :, span], mine_ref.at[:, :, span], mine_sem.at[chunk])

    lax.fori_loop(0, rows * chunks, a_step, 0)

    for line, (_, _, after) in enumerate(plans):
        if after:
            @pl.when(z == line)
            def _():
                for item in after:
                    relay(line, item)

    for chunk in range(chunks):
        swap(chunk).wait()
        keep_mine(chunk).wait()

    copy(0, here, 2, beside, True).wait_send()
    for line in range(lines):
        for part in (1, 2, 3):
            copy(part, line * 2 + y, 2, beside).wait_send()
        for part, origin in [(part, line * 2 + y) for part in (1, 2, 3, 0)] + [(0, line * 2 + 1 - y)]:
            @pl.when(has_up & (line <= z))
            def _():
                copy(part, origin, 0, up).wait_send()

            @pl.when(has_down & (line >= z))
            def _():
                copy(part, origin, 1, down).wait_send()


def gather_product(packed, place, ancestor_inverse, count, branch, size):
    rows = lax.axis_size("row")
    tile_rows, half_rows = ancestor_inverse.shape[1:]
    most = packed.shape[0]
    width = half_rows // rows
    chunk_rows = math.gcd(tile_rows, ROW_CHUNK)
    chunks = tile_rows // chunk_rows
    parts, plans = relay_plan(rows // 2, count, 2.82, 16.0 / chunks, chunks)
    column_shape = jax.ShapeDtypeStruct((4, 2, tile_rows, size), F32)
    return pl.pallas_call(
        functools.partial(gather_product_kernel, rows, parts, plans, size),
        out_shape=(
            jax.ShapeDtypeStruct((rows,) + packed.shape, F32), column_shape, column_shape,
        ),
        in_specs=[
            pl.BlockSpec(memory_space=pltpu.SMEM),
            pl.BlockSpec(memory_space=pl.ANY),
            pl.BlockSpec(memory_space=pl.ANY),
        ],
        out_specs=(pl.BlockSpec(memory_space=pl.ANY),) * 3,
        scratch_shapes=[
            pltpu.VMEM((count + 1,) + packed.shape[1:], F32),
            pltpu.VMEM((2, 2, chunk_rows, width), F32),
            pltpu.VMEM((3, width, 4 * size), BF16),
            pltpu.VMEM((3, width, 4 * size), BF16),
            pltpu.VMEM((3, tile_rows, 4 * size), F32),
            pltpu.VMEM((4, 2, tile_rows, size), F32),
            pltpu.SemaphoreType.DMA((4, rows, 3)),
            pltpu.SemaphoreType.DMA((4, rows)),
            pltpu.SemaphoreType.DMA,
            pltpu.SemaphoreType.DMA,
            pltpu.SemaphoreType.DMA((2,)),
            pltpu.SemaphoreType.DMA((chunks,)),
            pltpu.SemaphoreType.DMA((chunks,)),
            pltpu.SemaphoreType.DMA((chunks,)),
        ],
        compiler_params=pltpu.CompilerParams(
            collective_id=branch + 1, has_side_effects=True, vmem_limit_bytes=VMEM_BYTES
        ),
    )(place, packed, ancestor_inverse)


def wide(matrix):
    return jnp.concatenate([matrix[0], matrix[1]], axis=1)


def folded(product, size, transposed):
    return jnp.stack(
        [
            product[:size, :size] - product[size:, size:],
            product[:size, size:] + product[size:, :size],
        ]
    )


def contracted(left_side, right_side):
    return lax.dot_general(
        left_side, right_side, (((0,), (0,)), ((), ())),
        preferred_element_type=F32, precision=lax.Precision.HIGHEST,
    )


def finish_kernel(
    size, live_ref, own_ref, order_ref, source_ref,
    mine_ref, other_ref, link_ref, w0_ref, w1_ref, w2_ref, w3_ref,
    columns_ref, sums_ref,
):
    row = pl.program_id(0)
    windows = (w0_ref, w1_ref, w2_ref, w3_ref)

    @pl.when(row == 0)
    def _():
        sums_ref[...] = jnp.zeros_like(sums_ref)

    def window(slot):
        block = windows[slot][0, 0]
        return jnp.concatenate([block[:size], block[size:]], axis=1)

    for tree in range(2):
        child = tree + 2
        parent_at = order_ref[tree]
        child_at = order_ref[child]

        @pl.when(live_ref[tree, row] == 0)
        def _():
            columns_ref[parent_at] = jnp.zeros(columns_ref.shape[1:], F32)

        @pl.when(live_ref[child, row] == 0)
        def _():
            columns_ref[child_at] = jnp.zeros(columns_ref.shape[1:], F32)

        @pl.when(live_ref[tree, row] > 0)
        def _():
            columns_ref[parent_at] = -(mine_ref[tree] + other_ref[tree])

            @pl.when(own_ref[row] > 0)
            def _():
                sums_ref[tree] += folded(
                    contracted(window(tree), wide(columns_ref[parent_at])), size, True
                )

        @pl.when(live_ref[child, row] > 0)
        def _():
            parent = columns_ref[parent_at]
            linked = folded(
                matmul(jnp.concatenate([parent[0], parent[1]], axis=0), wide(link_ref[tree])),
                size, False,
            )
            columns_ref[child_at] = -(mine_ref[child] + other_ref[child] + linked)

            @pl.when(own_ref[row] > 0)
            def _():
                other_window = window(child)
                sums_ref[child] += folded(
                    contracted(wide(parent), other_window), size, True
                )
                sums_ref[tree + 4] += folded(
                    contracted(other_window, wide(columns_ref[child_at])), size, True
                )


def finish(mine, other, coupling, gathered, live, own, tree_order, source, size):
    rows = live.shape[1]

    def window_map(slot, g, live, own, order, source):
        return (source[0, slot, g], source[1, slot, g], 0, 0)

    return pl.pallas_call(
        functools.partial(finish_kernel, size),
        out_shape=(
            jax.ShapeDtypeStruct(mine.shape, F32),
            jax.ShapeDtypeStruct((6, 2, size, size), F32),
        ),
        grid_spec=pltpu.PrefetchScalarGridSpec(
            num_scalar_prefetch=4,
            grid=(rows,),
            in_specs=[
                pl.BlockSpec((4, 2, size, size), lambda g, *_: (0, 0, g, 0)),
                pl.BlockSpec((4, 2, size, size), lambda g, *_: (0, 0, g, 0)),
                pl.BlockSpec(coupling.shape, lambda g, *_: (0, 0, 0, 0)),
            ]
            + [
                pl.BlockSpec((1, 1, 2 * size, size), functools.partial(window_map, slot))
                for slot in range(4)
            ],
            out_specs=(
                pl.BlockSpec((4, 2, size, size), lambda g, *_: (0, 0, g, 0)),
                pl.BlockSpec((6, 2, size, size), lambda g, *_: (0, 0, 0, 0)),
            ),
        ),
        compiler_params=pltpu.CompilerParams(vmem_limit_bytes=VMEM_BYTES),
    )(live, own, tree_order, source, mine, other, coupling, gathered, gathered, gathered, gathered)


def sum_kernel(stages, part_ref, sum_ref, total, landed, send_sem, recv_sem):
    barrier = pltpu.get_barrier_semaphore()
    partners = []
    for axis, bit in stages:
        at = lax.axis_index(axis)
        mine = (at // (1 << bit)) % 2
        partners.append((axis, at + (1 << bit) * (1 - 2 * mine), mine))
    for axis, partner, _ in partners:
        pl.semaphore_signal(
            barrier, inc=1, device_id={axis: partner}, device_id_type=pl.DeviceIdType.MESH
        )
    pl.semaphore_wait(barrier, len(stages))

    total[...] = part_ref[...]
    length = part_ref.shape[0]
    start, landing = 0, 0
    spans = []
    for stage, (axis, partner, mine) in enumerate(partners):
        length = length // 2
        keep = pl.multiple_of(start + mine * length, 8)
        give = pl.multiple_of(start + (1 - mine) * length, 8)
        copy = pltpu.make_async_remote_copy(
            src_ref=total.at[pl.ds(give, length)],
            dst_ref=landed.at[pl.ds(landing, length)],
            send_sem=send_sem.at[stage],
            recv_sem=recv_sem.at[stage],
            device_id={axis: partner},
            device_id_type=pl.DeviceIdType.MESH,
        )
        copy.start()
        copy.wait()
        total[pl.ds(keep, length)] += landed[pl.ds(landing, length)]
        spans.append((keep, length))
        start, landing = keep, landing + length
    sum_ref[pl.ds(start, length)] = total[pl.ds(start, length)]
    for stage in reversed(range(len(stages))):
        axis, partner, _ = partners[stage]
        keep, length = spans[stage]
        copy = pltpu.make_async_remote_copy(
            src_ref=sum_ref.at[pl.ds(keep, length)],
            dst_ref=sum_ref.at[pl.ds(keep, length)],
            send_sem=send_sem.at[len(stages) + stage],
            recv_sem=recv_sem.at[len(stages) + stage],
            device_id={axis: partner},
            device_id_type=pl.DeviceIdType.MESH,
        )
        copy.start()
        copy.wait()


def summed(parts):
    stages = []
    for axis in ("col", "row"):
        count = lax.axis_size(axis)
        if count & (count - 1):
            return lax.psum(parts, ("row", "col"))
        stages += [(axis, bit) for bit in range(count.bit_length() - 1)]
    flat = parts.reshape(-1, parts.shape[-1])
    if flat.shape[0] % (8 << len(stages)) or not stages:
        return lax.psum(parts, ("row", "col"))
    total = pl.pallas_call(
        functools.partial(sum_kernel, stages),
        out_shape=jax.ShapeDtypeStruct(flat.shape, F32),
        in_specs=[pl.BlockSpec(memory_space=pltpu.VMEM)],
        out_specs=pl.BlockSpec(memory_space=pltpu.VMEM),
        scratch_shapes=[
            pltpu.VMEM(flat.shape, F32),
            pltpu.VMEM(flat.shape, F32),
            pltpu.SemaphoreType.DMA((2 * len(stages),)),
            pltpu.SemaphoreType.DMA((2 * len(stages),)),
        ],
        compiler_params=pltpu.CompilerParams(collective_id=0, has_side_effects=True),
    )(flat)
    return total.reshape(parts.shape)


def per_device_blocks(
    ancestor_inverse, factor_panels, diag_inverse, coupling, block_pattern, tree_order
):
    grid_row = lax.axis_index("row")
    grid_col = lax.axis_index("col")
    row_count = lax.axis_size("row")
    col_count = lax.axis_size("col")
    size = factor_panels.shape[3]
    tile_blocks = ancestor_inverse.shape[1] // size
    half_blocks = ancestor_inverse.shape[2] // size
    piece_blocks = factor_panels.shape[2] // size
    most = 4 * piece_blocks
    pattern = jnp.take(block_pattern, tree_order, axis=0) > 0
    pattern = jnp.concatenate([pattern[:2], pattern[2:] & pattern[:2]], axis=0)
    pattern = pattern.astype(jnp.int32)
    pieces = pattern.reshape(4, col_count, row_count, piece_blocks).transpose(1, 2, 0, 3)
    flat = pieces.reshape(col_count, row_count, most)
    position = (jnp.cumsum(flat, axis=2) - flat).reshape(pieces.shape)
    counts = jnp.sum(flat, axis=2)
    largest = jnp.max(counts)
    own_flat = flat[grid_col, grid_row]
    own_list = jnp.argsort(1 - own_flat, stable=True).astype(jnp.int32)
    supernode = jnp.take(tree_order, own_list // piece_blocks)
    block = own_list % piece_blocks
    half_live = lax.dynamic_slice_in_dim(pattern, grid_col * half_blocks, half_blocks, 1)
    live_rows = lax.dynamic_slice_in_dim(pattern, grid_row * tile_blocks, tile_blocks, 1)
    half_position = position[grid_col].transpose(1, 0, 2).reshape(4, half_blocks)
    tile_at = grid_row * tile_blocks + jnp.arange(tile_blocks, dtype=jnp.int32)
    own = (tile_at // half_blocks == grid_col).astype(jnp.int32)
    local = tile_at % half_blocks
    window_source = jnp.stack(
        [
            jnp.broadcast_to((local // piece_blocks)[None, :], (4, tile_blocks)),
            jnp.take(half_position, local, axis=1),
        ]
    ).astype(jnp.int32)

    packed = pack(factor_panels, supernode, block, size)
    half_pieces = pieces[grid_col]
    place = jnp.where(half_pieces > 0, position[grid_col] + 1, 0).astype(jnp.int32).reshape(-1)
    least = (most + 1) // 2
    sizes = sorted({*range(least + 2, min(least + 7, most)), least + (most - least) * 2 // 3, most})

    def branch(at):
        return lambda blocks: gather_product(blocks, place, ancestor_inverse, sizes[at], at, size)

    choice = jnp.sum((largest > jnp.array(sizes[:-1])).astype(jnp.int32))
    gathered, mine, other = lax.switch(choice, [branch(at) for at in range(len(sizes))], packed)
    window_source = jnp.minimum(
        window_source, jnp.array([row_count, most], jnp.int32)[:, None, None] - 1
    )
    inverse_panels, sums = finish(
        mine, other, coupling, gathered, live_rows, own, tree_order, window_source, size
    )
    totals = summed(sums)
    diag_blocks = jnp.take(diag_inverse, tree_order, axis=0)
    parent_diag = [diag_blocks[tree] - totals[tree] for tree in range(2)]
    crosses = [
        -(totals[2 + tree] + multiply(parent_diag[tree], coupling[tree])) for tree in range(2)
    ]
    child_diag = [
        diag_blocks[tree + 2] - totals[4 + tree] - multiply(flipped(coupling[tree]), crosses[tree])
        for tree in range(2)
    ]
    all_diag = jnp.stack(parent_diag + child_diag)
    inverse_diagonal = jnp.take(all_diag, jnp.argsort(tree_order), axis=0)
    return (inverse_panels, inverse_diagonal, jnp.stack(crosses))


def per_device(ancestor_inverse, factor_panels, diag_inverse, coupling, block_pattern, tree_order):
    size = factor_panels.shape[3]
    rows = lax.axis_size("row")
    whole_blocks = math.gcd(ancestor_inverse.shape[1], factor_panels.shape[2]) % size == 0
    paired = rows % 2 == 0 and rows >= 4 and lax.axis_size("col") == 2
    blocks = whole_blocks and size % 128 == 0 and paired and ancestor_inverse.shape[1] <= 1536
    run = per_device_blocks if blocks else per_device_dense
    return run(ancestor_inverse, factor_panels, diag_inverse, coupling, block_pattern, tree_order)


def solution(mesh):
    return jax.shard_map(
        per_device,
        mesh=mesh,
        in_specs=(
            P(None, ("pole", "row"), "col"),
            P(None, None, ("pole", "col", "row"), None),
            P("pole", None, None, None),
            P("pole", None, None, None),
            P(),
            P(),
        ),
        out_specs=(
            P(None, None, ("pole", "row"), None),
            P("pole", None, None, None),
            P("pole", None, None, None),
        ),
        check_vma=False,
    )
```

```python
import functools
import math

import jax
import jax.numpy as jnp
from jax import lax
from jax.experimental import pallas as pl
from jax.experimental.pallas import tpu as pltpu
from jax.sharding import PartitionSpec as P

BF16 = jnp.bfloat16
F32 = jnp.float32
GROUP = 8
VMEM_BYTES = 64 * 1024 * 1024 - 256 * 1024


def swapped(block, axis, bit):
    count = lax.axis_size(axis)
    route = []
    for low in range(count):
        high = low | 1 << bit
        if high != low and high < count:
            route += [(low, high), (high, low)]
    return lax.ppermute(block, axis, route)


def matmul(left_side, right_side):
    return jnp.dot(
        left_side, right_side, preferred_element_type=jnp.float32, precision=lax.Precision.HIGHEST
    )


def multiply(left_side, right_side):
    real_part = matmul(left_side[0], right_side[0]) - matmul(left_side[1], right_side[1])
    imag_part = matmul(left_side[0], right_side[1]) + matmul(left_side[1], right_side[0])
    return jnp.stack([real_part, imag_part])


def flipped(matrix):
    return jnp.swapaxes(matrix, 1, 2)


def row_masks(pattern_eff, first_row, row_count, block_rows):
    row_index = first_row + jnp.arange(row_count, dtype=jnp.int32)
    blocks = row_index // block_rows
    onehot = (blocks[:, None] == jnp.arange(pattern_eff.shape[1], dtype=jnp.int32)[None, :]).astype(
        jnp.float32
    )
    return matmul(pattern_eff, onehot.T)


def per_device_dense(ancestor_inverse, factor_panels, diag_inverse, coupling, block_pattern, tree_order):
    grid_row = lax.axis_index("row")
    grid_col = lax.axis_index("col")
    tile_rows = ancestor_inverse.shape[1]
    half_rows = ancestor_inverse.shape[2]
    piece_rows = factor_panels.shape[2]
    block_rows = factor_panels.shape[3]
    super_count = factor_panels.shape[0]
    share_rows = tile_rows // 2
    sorted_pattern = jnp.take(block_pattern, tree_order, axis=0).astype(jnp.float32)
    pattern_eff = jnp.concatenate(
        [sorted_pattern[:2], sorted_pattern[2:] * sorted_pattern[:2]], axis=0
    )
    source_mask = row_masks(
        pattern_eff, grid_col * half_rows + grid_row * piece_rows, piece_rows, block_rows
    )
    target_mask = row_masks(pattern_eff, grid_row * tile_rows, tile_rows, block_rows)
    panels = jnp.take(factor_panels, tree_order, axis=0) * source_mask[:, None, :, None]
    diag_blocks = jnp.take(diag_inverse, tree_order, axis=0)
    columns = []
    products = []
    for tree_slot in range(super_count):
        gathered = lax.all_gather(panels[tree_slot], "row", axis=1, tiled=True)
        columns.append(gathered)
        products.append(lax.psum(multiply(ancestor_inverse, gathered), "col"))
    own_flag = (grid_row * tile_rows // half_rows == grid_col).astype(jnp.float32)
    offset = jnp.clip(grid_row * tile_rows - grid_col * half_rows, 0, half_rows - tile_rows)
    own_windows = jnp.stack(
        [
            lax.dynamic_slice_in_dim(column_set, offset, tile_rows, 1) * own_flag
            for column_set in columns
        ]
    )
    partner_windows = swapped(own_windows, "col", 0)
    tile_windows = own_windows + partner_windows

    def share(matrix):
        return lax.dynamic_slice_in_dim(matrix, grid_col * share_rows, share_rows, 1)

    windows = [share(tile_windows[tree_slot]) for tree_slot in range(super_count)]
    parent_cols = [
        -target_mask[tree_slot][None, :, None] * products[tree_slot] for tree_slot in range(2)
    ]
    child_cols = [
        -target_mask[tree_slot + 2][None, :, None]
        * (products[tree_slot + 2] + multiply(parent_cols[tree_slot], coupling[tree_slot]))
        for tree_slot in range(2)
    ]
    parent_local = [
        multiply(flipped(windows[tree_slot]), share(parent_cols[tree_slot]))
        for tree_slot in range(2)
    ]
    cross_local = [
        multiply(flipped(share(parent_cols[tree_slot])), windows[tree_slot + 2])
        for tree_slot in range(2)
    ]
    child_local = [
        multiply(flipped(windows[tree_slot + 2]), share(child_cols[tree_slot]))
        for tree_slot in range(2)
    ]
    parent_sums = lax.psum(jnp.stack(parent_local), ("row", "col"))
    parent_diag = [diag_blocks[tree_slot] - parent_sums[tree_slot] for tree_slot in range(2)]
    child_totals = lax.psum(jnp.stack(cross_local + child_local), ("row", "col"))
    crosses = [
        -(child_totals[tree_slot] + multiply(parent_diag[tree_slot], coupling[tree_slot]))
        for tree_slot in range(2)
    ]
    child_sums = [child_totals[2 + tree_slot] for tree_slot in range(2)]
    child_diag = [
        diag_blocks[tree_slot + 2]
        - child_sums[tree_slot]
        - multiply(flipped(coupling[tree_slot]), crosses[tree_slot])
        for tree_slot in range(2)
    ]
    all_cols = jnp.stack(parent_cols + child_cols)
    all_diag = jnp.stack(parent_diag + child_diag)
    inverse_panels = jnp.zeros_like(all_cols).at[tree_order].set(all_cols)
    inverse_diagonal = jnp.zeros_like(all_diag).at[tree_order].set(all_diag)
    return (inverse_panels, inverse_diagonal, jnp.stack(crosses))


def halves(value):
    high = value.astype(BF16)
    return high, (value - high.astype(F32)).astype(BF16)


def prepare_kernel(
    sizes, pattern_ref, order_ref, panels_ref,
    place_ref, window_ref, live_ref, choice_ref, packed_ref,
    held, load_sem, keep_sem,
):
    grid_row, grid_col = lax.axis_index("row"), lax.axis_index("col")
    rows, cols = lax.axis_size("row"), lax.axis_size("col")
    size = panels_ref.shape[3]
    blocks = panels_ref.shape[2] // size
    most = 4 * blocks
    tile_blocks = pattern_ref.shape[1] // rows
    half_blocks = rows * blocks
    order = [order_ref[slot] for slot in range(4)]

    def live_slots(block):
        marks = [pattern_ref[order[slot], block] for slot in range(4)]
        return [
            marks[0] > 0, marks[1] > 0,
            (marks[2] > 0) & (marks[0] > 0), (marks[3] > 0) & (marks[1] > 0),
        ]

    own_start = (grid_col * rows + grid_row) * blocks
    own_live = [live_slots(own_start + block) for block in range(blocks)]

    def load(slot, block, at):
        return pltpu.make_async_copy(
            panels_ref.at[order[slot], :, pl.ds(block * size, size), :], held.at[at], load_sem.at[at]
        )

    at = jnp.int32(0)
    for slot in range(4):
        for block in range(blocks):
            flag = own_live[block][slot]

            @pl.when(flag)
            def _():
                load(slot, block, at).start()

            at = at + flag.astype(jnp.int32)
    own_count = at

    def count_piece(piece, largest):
        total = jnp.int32(0)
        for block in range(blocks):
            for flag in live_slots(piece * blocks + block):
                total = total + flag.astype(jnp.int32)
        return jnp.maximum(largest, total)

    largest = lax.fori_loop(0, rows * cols, count_piece, jnp.int32(0))
    choice = jnp.int32(0)
    for limit in sizes[:-1]:
        choice = choice + (largest > limit).astype(jnp.int32)
    choice_ref[0] = choice

    def place_piece(piece, _):
        live = [live_slots((grid_col * rows + piece) * blocks + block) for block in range(blocks)]
        spot = jnp.int32(1)
        for slot in range(4):
            for block in range(blocks):
                flag = live[block][slot]
                place_ref[piece * most + slot * blocks + block] = jnp.where(flag, spot, 0)
                spot = spot + flag.astype(jnp.int32)
        return 0

    lax.fori_loop(0, rows, place_piece, 0)

    def window_row(row, _):
        block = grid_row * tile_blocks + row
        here = (block // half_blocks == grid_col).astype(jnp.int32)
        local = block % half_blocks
        piece, inside = local // blocks, local % blocks
        for slot, flag in enumerate(live_slots(block)):
            live_ref[slot, row] = flag.astype(jnp.int32)
            spot = place_ref[piece * most + slot * blocks + inside]
            window_ref[slot, row] = jnp.where(
                (here > 0) & (spot > 0), piece * most + spot - 1, 0
            )
        live_ref[4, row] = here
        return 0

    lax.fori_loop(0, tile_blocks, window_row, 0)

    def keep(at):
        return pltpu.make_async_copy(held.at[at], packed_ref.at[at], keep_sem.at[at])

    @pl.loop(0, own_count)
    def _(at):
        load(0, 0, at).wait()
        keep(at).start()

    @pl.loop(0, own_count)
    def _(at):
        keep(at).wait()


def prepare(block_pattern, tree_order, factor_panels, sizes):
    rows = lax.axis_size("row")
    size = factor_panels.shape[3]
    most = 4 * (factor_panels.shape[2] // size)
    tile_blocks = block_pattern.shape[1] // rows
    smem = pl.BlockSpec(memory_space=pltpu.SMEM)
    return pl.pallas_call(
        functools.partial(prepare_kernel, sizes),
        out_shape=(
            jax.ShapeDtypeStruct((rows * most,), jnp.int32),
            jax.ShapeDtypeStruct((4, tile_blocks), jnp.int32),
            jax.ShapeDtypeStruct((5, tile_blocks), jnp.int32),
            jax.ShapeDtypeStruct((1,), jnp.int32),
            jax.ShapeDtypeStruct((most, 2, size, size), F32),
        ),
        in_specs=[smem, smem, pl.BlockSpec(memory_space=pl.ANY)],
        out_specs=(smem, smem, smem, smem, pl.BlockSpec(memory_space=pl.ANY)),
        scratch_shapes=[
            pltpu.VMEM((most, 2, size, size), F32),
            pltpu.SemaphoreType.DMA((most,)),
            pltpu.SemaphoreType.DMA((most,)),
        ],
    )(block_pattern, tree_order, factor_panels)


ROW_CHUNK = 256


def relay_plan(lines, count, block_us, unit_us, units):
    first = max(1, round(count / 6))
    rest = count - first
    cuts = [first + rest * at // 3 for at in range(4)]
    parts = [(0, first)] + [(cuts[at], cuts[at + 1]) for at in range(3)]
    cost = [(high - low) * block_us for low, high in parts]
    beside_time = cost[0]

    def stream(own_items, forwarded):
        clock, landed = 0.0, {}
        for item, ready in own_items + forwarded:
            clock = max(clock, ready) + cost[item[2]]
            landed[item] = clock
        return landed

    climbs = {}
    for way in (1, -1):
        order = range(lines) if way == 1 else range(lines - 1, -1, -1)
        before = {}
        for z in order:
            climbs[way, z] = before
            own = [((z, 0, part), 0.0) for part in (1, 2, 3, 0)] + [((z, 1, 0), beside_time)]
            before = stream(own, sorted(before.items(), key=lambda pair: pair[1]))
    plans = []
    for z in range(lines):
        landed = {**climbs[1, z], **climbs[-1, z]}
        crossing = sorted(
            ((item, when) for item, when in landed.items() if item[1] == 0 and item[2] > 0),
            key=lambda pair: pair[1],
        )
        across = stream([((z, 0, part), 0.0) for part in (0, 1, 2, 3)], crossing)
        ready = {(z, 0): 0.0}
        for item, when in landed.items():
            key = item[:2]
            ready[key] = max(ready.get(key, 0.0), when)
        for item, when in across.items():
            key = (item[0], 1)
            ready[key] = max(ready.get(key, 0.0), when)
        events = sorted([((z, 1, 0), beside_time)] + list(landed.items()), key=lambda pair: pair[1])
        pieces = sorted(ready, key=lambda key: ready[key])
        clock, at, before_unit, after = 0.0, 0, {}, []
        for turn, piece in enumerate(pieces):
            for unit in range(units):
                start = max(clock, ready[piece]) if unit == 0 else clock
                while at < len(events) and events[at][1] <= start:
                    before_unit.setdefault(turn * units + unit, []).append(events[at][0])
                    at += 1
                clock = start + unit_us
        after = [event for event, _ in events[at:]]
        plans.append((pieces, before_unit, after))
    return parts, plans


def gather_product_kernel(
    rows, parts, plans, size,
    place_ref, own_ref, a_ref, all_ref, mine_ref, other_ref,
    staged, a_stage, b_high, b_low, acc, mine,
    send_sem, recv_sem, load_sem, keep_sem, a_sem, mine_sem, swap_send, swap_recv,
):
    here = lax.axis_index("row")
    sibling = 1 - lax.axis_index("col")
    lines = rows // 2
    z, y = here // 2, here % 2
    count = parts[-1][1]
    chunk_rows = a_stage.shape[2]
    chunks = a_ref.shape[1] // chunk_rows
    width = b_high.shape[1]
    blocks = width // size
    beside = z * 2 + (1 - y)
    up, down = here + 2, here - 2
    has_up, has_down = z < lines - 1, z > 0

    def copy(part, origin, way, target, own=False):
        low, high = parts[part]
        span = pl.ds(low, high - low)
        return pltpu.make_async_remote_copy(
            src_ref=own_ref.at[span] if own else all_ref.at[origin, span],
            dst_ref=all_ref.at[origin, span],
            send_sem=send_sem.at[part, origin, way],
            recv_sem=recv_sem.at[part, origin],
            device_id={"row": target},
            device_id_type=pl.DeviceIdType.MESH,
        )

    def arrived(part, origin):
        copy(part, origin, 0, beside).wait_recv()

    barrier = pltpu.get_barrier_semaphore()

    def greet(target):
        pl.semaphore_signal(barrier, inc=1, device_id=target, device_id_type=pl.DeviceIdType.MESH)

    greet({"row": beside})
    greet({"col": sibling})

    @pl.when(has_up)
    def _():
        greet({"row": up})

    @pl.when(has_down)
    def _():
        greet({"row": down})

    pl.semaphore_wait(barrier, 2 + has_up.astype(jnp.int32) + has_down.astype(jnp.int32))

    copy(0, here, 2, beside, True).start()
    for part in (1, 2, 3, 0):
        @pl.when(has_up)
        def _():
            copy(part, here, 0, up, True).start()

        @pl.when(has_down)
        def _():
            copy(part, here, 1, down, True).start()

        if part:
            copy(part, here, 2, beside, True).start()

    def origin_of(turn):
        origin = here
        for line, (pieces, _, _) in enumerate(plans):
            for at, (from_line, side) in enumerate(pieces):
                origin = jnp.where(
                    (z == line) & (turn == at), from_line * 2 + (y if side == 0 else 1 - y), origin
                )
        return origin

    def a_copy(step, origin):
        chunk = step % chunks
        return pltpu.make_async_copy(
            a_ref.at[
                :,
                pl.ds(pl.multiple_of(chunk * chunk_rows, 8), chunk_rows),
                pl.ds(pl.multiple_of(origin * width, 128), width),
            ],
            a_stage.at[step % 2],
            a_sem.at[step % 2],
        )

    a_copy(0, origin_of(0)).start()
    a_copy(1, origin_of(1 // chunks)).start()
    acc[...] = jnp.zeros_like(acc)
    staged[0] = jnp.zeros(staged.shape[1:], F32)

    def relay(line, item):
        from_line, side, part = item
        origin = from_line * 2 + (y if side == 0 else 1 - y)
        arrived(part, origin)
        if from_line == line:
            ways = ([0] if line < lines - 1 else []) + ([1] if line > 0 else [])
        elif from_line < line:
            ways = [0] if line < lines - 1 else []
        else:
            ways = [1] if line > 0 else []
        for way in ways:
            copy(part, origin, way, up if way == 0 else down).start()
        if side == 0 and part:
            copy(part, origin, 2, beside).start()

    def a_step(step, _):
        turn, chunk = step // chunks, step % chunks
        for line, (pieces, before_unit, _) in enumerate(plans):
            @pl.when(z == line)
            def _():
                for at in sorted(before_unit):
                    @pl.when(step == at)
                    def _():
                        for item in before_unit[at]:
                            relay(line, item)

        @pl.when(chunk == 0)
        def _():
            for line, (pieces, _, _) in enumerate(plans):
                for at, (from_line, side) in enumerate(pieces):
                    if side == 1:
                        @pl.when((z == line) & (turn == at))
                        def _():
                            for part in (1, 2, 3):
                                arrived(part, from_line * 2 + (1 - y))

            origin = origin_of(turn)

            @pl.when(turn == 0)
            def _():
                load = pltpu.make_async_copy(own_ref.at[pl.ds(0, count)], staged.at[pl.ds(1, count)], load_sem)
                load.start()
                load.wait()
                pltpu.make_async_copy(
                    staged.at[pl.ds(1, count)], all_ref.at[here, pl.ds(0, count)], keep_sem
                ).start()

            @pl.when(turn == 1)
            def _():
                pltpu.make_async_copy(
                    staged.at[pl.ds(1, count)], all_ref.at[here, pl.ds(0, count)], keep_sem
                ).wait()

            @pl.when(turn > 0)
            def _():
                load = pltpu.make_async_copy(
                    all_ref.at[origin, pl.ds(0, count)], staged.at[pl.ds(1, count)], load_sem
                )
                load.start()
                load.wait()

            def spread(block, _):
                span = pl.ds(pl.multiple_of(block * size, size), size)
                for slot in range(4):
                    value = staged[place_ref[origin * (4 * blocks) + slot * blocks + block]]
                    for kind, term in enumerate((value[0], value[1], value[0] + value[1])):
                        high, low = halves(term)
                        b_high[kind, span, slot * size:(slot + 1) * size] = high
                        b_low[kind, span, slot * size:(slot + 1) * size] = low
                return 0

            lax.fori_loop(0, blocks, spread, 0)

        a_copy(step, here).wait()
        span = pl.ds(pl.multiple_of(chunk * chunk_rows, 8), chunk_rows)
        real, imag = a_stage[step % 2, 0], a_stage[step % 2, 1]
        for kind, term in enumerate((real, imag, real + imag)):
            high, low = halves(term)
            acc[kind, span, :] += jnp.dot(
                jnp.concatenate([high, low, high], axis=1),
                jnp.concatenate([b_high[kind], b_high[kind], b_low[kind]], axis=0),
                preferred_element_type=F32,
            )

        @pl.when(step + 2 < rows * chunks)
        def _():
            a_copy(step + 2, origin_of((step + 2) // chunks)).start()

        @pl.when(turn == rows - 1)
        def _():
            for slot in range(4):
                columns = slice(slot * size, (slot + 1) * size)
                first, second = acc[0, span, columns], acc[1, span, columns]
                mine[slot, 0, span] = first - second
                mine[slot, 1, span] = acc[2, span, columns] - first - second
            swap(chunk).start()
            keep_mine(chunk).start()

        return 0

    def swap(chunk):
        span = pl.ds(pl.multiple_of(chunk * chunk_rows, 8), chunk_rows)
        return pltpu.make_async_remote_copy(
            src_ref=mine.at[:, :, span],
            dst_ref=other_ref.at[:, :, span],
            send_sem=swap_send.at[chunk],
            recv_sem=swap_recv.at[chunk],
            device_id={"col": sibling},
            device_id_type=pl.DeviceIdType.MESH,
        )

    def keep_mine(chunk):
        span = pl.ds(pl.multiple_of(chunk * chunk_rows, 8), chunk_rows)
        return pltpu.make_async_copy(mine.at[:, :, span], mine_ref.at[:, :, span], mine_sem.at[chunk])

    lax.fori_loop(0, rows * chunks, a_step, 0)

    for line, (_, _, after) in enumerate(plans):
        if after:
            @pl.when(z == line)
            def _():
                for item in after:
                    relay(line, item)

    for chunk in range(chunks):
        swap(chunk).wait()
        keep_mine(chunk).wait()

    copy(0, here, 2, beside, True).wait_send()
    for line in range(lines):
        for part in (1, 2, 3):
            copy(part, line * 2 + y, 2, beside).wait_send()
        for part, origin in [(part, line * 2 + y) for part in (1, 2, 3, 0)] + [(0, line * 2 + 1 - y)]:
            @pl.when(has_up & (line <= z))
            def _():
                copy(part, origin, 0, up).wait_send()

            @pl.when(has_down & (line >= z))
            def _():
                copy(part, origin, 1, down).wait_send()


def gather_product(packed, place, ancestor_inverse, count, branch, size):
    rows = lax.axis_size("row")
    tile_rows, half_rows = ancestor_inverse.shape[1:]
    most = packed.shape[0]
    width = half_rows // rows
    chunk_rows = math.gcd(tile_rows, ROW_CHUNK)
    chunks = tile_rows // chunk_rows
    parts, plans = relay_plan(rows // 2, count, 2.82, 16.0 / chunks, chunks)
    column_shape = jax.ShapeDtypeStruct((4, 2, tile_rows, size), F32)
    return pl.pallas_call(
        functools.partial(gather_product_kernel, rows, parts, plans, size),
        out_shape=(
            jax.ShapeDtypeStruct((rows,) + packed.shape, F32), column_shape, column_shape,
        ),
        in_specs=[
            pl.BlockSpec(memory_space=pltpu.SMEM),
            pl.BlockSpec(memory_space=pl.ANY),
            pl.BlockSpec(memory_space=pl.ANY),
        ],
        out_specs=(pl.BlockSpec(memory_space=pl.ANY),) * 3,
        scratch_shapes=[
            pltpu.VMEM((count + 1,) + packed.shape[1:], F32),
            pltpu.VMEM((2, 2, chunk_rows, width), F32),
            pltpu.VMEM((3, width, 4 * size), BF16),
            pltpu.VMEM((3, width, 4 * size), BF16),
            pltpu.VMEM((3, tile_rows, 4 * size), F32),
            pltpu.VMEM((4, 2, tile_rows, size), F32),
            pltpu.SemaphoreType.DMA((4, rows, 3)),
            pltpu.SemaphoreType.DMA((4, rows)),
            pltpu.SemaphoreType.DMA,
            pltpu.SemaphoreType.DMA,
            pltpu.SemaphoreType.DMA((2,)),
            pltpu.SemaphoreType.DMA((chunks,)),
            pltpu.SemaphoreType.DMA((chunks,)),
            pltpu.SemaphoreType.DMA((chunks,)),
        ],
        compiler_params=pltpu.CompilerParams(
            collective_id=branch + 1, has_side_effects=True, vmem_limit_bytes=VMEM_BYTES
        ),
    )(place, packed, ancestor_inverse)


def wide(matrix):
    return jnp.concatenate([matrix[0], matrix[1]], axis=1)


def folded(product, size):
    return jnp.stack(
        [
            product[:size, :size] - product[size:, size:],
            product[:size, size:] + product[size:, :size],
        ]
    )


def contracted(left_side, right_side):
    return lax.dot_general(
        left_side, right_side, (((0,), (0,)), ((), ())), preferred_element_type=F32
    )


def tripled(value, axis, right):
    high, low = halves(value)
    return jnp.concatenate([high, high, low] if right else [high, low, high], axis=axis)


def finish_kernel(
    size, live_ref, order_ref, window_at_ref,
    mine_ref, other_ref, link_ref, w0_ref, w1_ref, w2_ref, w3_ref,
    columns_ref, sums_ref, acc,
):
    row = pl.program_id(0)
    windows = (w0_ref, w1_ref, w2_ref, w3_ref)

    @pl.when(row == 0)
    def _():
        acc[...] = jnp.zeros_like(acc)

    for tree in range(2):
        child = tree + 2
        parent_at = order_ref[tree]
        child_at = order_ref[child]

        @pl.when(live_ref[tree, row] == 0)
        def _():
            columns_ref[parent_at] = jnp.zeros(columns_ref.shape[1:], F32)

        @pl.when(live_ref[child, row] == 0)
        def _():
            columns_ref[child_at] = jnp.zeros(columns_ref.shape[1:], F32)

        @pl.when(live_ref[tree, row] > 0)
        def _():
            columns_ref[parent_at] = -(mine_ref[tree] + other_ref[tree])

        @pl.when(live_ref[child, row] > 0)
        def _():
            parent = columns_ref[parent_at]
            linked = jnp.dot(
                tripled(jnp.concatenate([parent[0], parent[1]], axis=0), 1, False),
                tripled(wide(link_ref[tree]), 0, True),
                preferred_element_type=F32,
            )
            columns_ref[child_at] = -(mine_ref[child] + other_ref[child] + folded(linked, size))

        @pl.when((live_ref[4, row] > 0) & (live_ref[tree, row] > 0))
        def _():
            parent = tripled(wide(columns_ref[parent_at]), 0, True)

            @pl.when(live_ref[child, row] == 0)
            def _():
                acc[tree, :2 * size, :2 * size] += contracted(
                    tripled(wide(windows[tree][0]), 0, False), parent
                )

            @pl.when(live_ref[child, row] > 0)
            def _():
                acc[tree] += contracted(
                    jnp.concatenate(
                        [tripled(wide(windows[at][0]), 0, False) for at in (tree, child)], axis=1
                    ),
                    jnp.concatenate(
                        [parent, tripled(wide(columns_ref[child_at]), 0, True)], axis=1
                    ),
                )

    @pl.when(row == pl.num_programs(0) - 1)
    def _():
        for tree in range(2):
            for kind, (high, wide_at) in enumerate(((0, 0), (1, 0), (1, 1))):
                block = acc[
                    tree, 2 * size * high:2 * size * (high + 1),
                    2 * size * wide_at:2 * size * (wide_at + 1),
                ]
                sums_ref[2 * kind + tree] = folded(block, size)


def finish(mine, other, coupling, gathered, live, tree_order, window_at, size):
    rows = live.shape[1]
    gathered = gathered.reshape((-1,) + gathered.shape[2:])

    def window_map(slot, g, live, order, window_at):
        return (window_at[slot, g], 0, 0, 0)

    return pl.pallas_call(
        functools.partial(finish_kernel, size),
        out_shape=(
            jax.ShapeDtypeStruct(mine.shape, F32),
            jax.ShapeDtypeStruct((6, 2, size, size), F32),
        ),
        grid_spec=pltpu.PrefetchScalarGridSpec(
            num_scalar_prefetch=3,
            grid=(rows,),
            in_specs=[
                pl.BlockSpec((4, 2, size, size), lambda g, *_: (0, 0, g, 0)),
                pl.BlockSpec((4, 2, size, size), lambda g, *_: (0, 0, g, 0)),
                pl.BlockSpec(coupling.shape, lambda g, *_: (0, 0, 0, 0)),
            ]
            + [
                pl.BlockSpec((1, 2, size, size), functools.partial(window_map, slot))
                for slot in range(4)
            ],
            out_specs=(
                pl.BlockSpec((4, 2, size, size), lambda g, *_: (0, 0, g, 0)),
                pl.BlockSpec((6, 2, size, size), lambda g, *_: (0, 0, 0, 0)),
            ),
            scratch_shapes=[pltpu.VMEM((2, 4 * size, 4 * size), F32)],
        ),
        compiler_params=pltpu.CompilerParams(vmem_limit_bytes=VMEM_BYTES),
    )(live, tree_order, window_at, mine, other, coupling, gathered, gathered, gathered, gathered)


def close_kernel(size, order_ref, totals_ref, diag_ref, link_ref, diagonal_ref, cross_ref):
    def times(left_side, right_side):
        return folded(
            matmul(jnp.concatenate([left_side[0], left_side[1]], axis=0), wide(right_side)), size
        )

    for tree in range(2):
        parent_at, child_at = order_ref[tree], order_ref[tree + 2]
        link = link_ref[tree]
        parent = diag_ref[parent_at] - totals_ref[tree]
        crossed = jnp.stack([totals_ref[2 + tree, part].T for part in range(2)])
        cross = -(crossed + times(parent, link))
        turned = jnp.stack([link[part].T for part in range(2)])
        diagonal_ref[parent_at] = parent
        cross_ref[tree] = cross
        diagonal_ref[child_at] = diag_ref[child_at] - totals_ref[4 + tree] - times(turned, cross)


def close(totals, diag_inverse, coupling, tree_order, size):
    whole = pl.BlockSpec(memory_space=pltpu.VMEM)
    return pl.pallas_call(
        functools.partial(close_kernel, size),
        out_shape=(
            jax.ShapeDtypeStruct(diag_inverse.shape, F32),
            jax.ShapeDtypeStruct(coupling.shape, F32),
        ),
        in_specs=[pl.BlockSpec(memory_space=pltpu.SMEM), whole, whole, whole],
        out_specs=(whole, whole),
    )(tree_order, totals, diag_inverse, coupling)


def sum_kernel(routes, part_ref, sum_ref, total, landed, send_sem, recv_sem):
    barrier = pltpu.get_barrier_semaphore()

    def partner_of(axis, bit):
        at = lax.axis_index(axis)
        mine = (at // (1 << bit)) % 2
        return at + (1 << bit) * (1 - 2 * mine), mine

    for axis, bit in routes[0]:
        pl.semaphore_signal(
            barrier, inc=1, device_id={axis: partner_of(axis, bit)[0]},
            device_id_type=pl.DeviceIdType.MESH,
        )
    pl.semaphore_wait(barrier, len(routes[0]))

    def copy(route, stage, source, source_at, target, target_at, length):
        axis, bit = routes[route][stage % len(routes[route])]
        return pltpu.make_async_remote_copy(
            src_ref=source.at[pl.ds(source_at, length)],
            dst_ref=target.at[pl.ds(target_at, length)],
            send_sem=send_sem.at[route, stage],
            recv_sem=recv_sem.at[route, stage],
            device_id={axis: partner_of(axis, bit)[0]},
            device_id_type=pl.DeviceIdType.MESH,
        )

    total[...] = part_ref[...]
    stages = len(routes[0])
    whole = part_ref.shape[0] // len(routes)
    length = whole
    starts = [whole * route for route in range(len(routes))]
    landings = list(starts)
    spans = []
    for stage in range(stages):
        length = length // 2
        copies, keeps = [], []
        for route in range(len(routes)):
            mine = partner_of(*routes[route][stage])[1]
            keep = pl.multiple_of(starts[route] + mine * length, 8)
            give = pl.multiple_of(starts[route] + (1 - mine) * length, 8)
            move = copy(route, stage, total, give, landed, landings[route], length)
            move.start()
            copies.append(move)
            keeps.append(keep)
        for route in range(len(routes)):
            copies[route].wait()
            landing = landings[route]
            total[pl.ds(keeps[route], length)] += landed[pl.ds(landing, length)]
            landings[route] = landing + length
        starts = keeps
        spans.append((keeps, length))
    for route in range(len(routes)):
        sum_ref[pl.ds(starts[route], length)] = total[pl.ds(starts[route], length)]
    for stage in reversed(range(stages)):
        keeps, length = spans[stage]
        copies = []
        for route in range(len(routes)):
            keep = keeps[route]
            move = copy(route, stages + stage, sum_ref, keep, sum_ref, keep, length)
            move.start()
            copies.append(move)
        for move in copies:
            move.wait()


def summed(parts):
    stages = []
    for axis in ("col", "row"):
        count = lax.axis_size(axis)
        if count & (count - 1):
            return lax.psum(parts, ("row", "col"))
        stages += [(axis, bit) for bit in range(count.bit_length() - 1)]
    flat = parts.reshape(-1, parts.shape[-1])
    if flat.shape[0] % (16 << len(stages)) or len(stages) < 3:
        return lax.psum(parts, ("row", "col"))
    routes = (tuple(stages), (stages[0], *stages[2:], stages[1]))
    total = pl.pallas_call(
        functools.partial(sum_kernel, routes),
        out_shape=jax.ShapeDtypeStruct(flat.shape, F32),
        in_specs=[pl.BlockSpec(memory_space=pltpu.VMEM)],
        out_specs=pl.BlockSpec(memory_space=pltpu.VMEM),
        scratch_shapes=[
            pltpu.VMEM(flat.shape, F32),
            pltpu.VMEM(flat.shape, F32),
            pltpu.SemaphoreType.DMA((2, 2 * len(stages))),
            pltpu.SemaphoreType.DMA((2, 2 * len(stages))),
        ],
        compiler_params=pltpu.CompilerParams(collective_id=0, has_side_effects=True),
    )(flat)
    return total.reshape(parts.shape)


def per_device_blocks(
    ancestor_inverse, factor_panels, diag_inverse, coupling, block_pattern, tree_order
):
    size = factor_panels.shape[3]
    most = 4 * (factor_panels.shape[2] // size)
    least = (most + 1) // 2
    sizes = sorted({*range(least + 2, min(least + 7, most)), least + (most - least) * 2 // 3, most})
    place, window_at, live, choice, packed = prepare(
        block_pattern, tree_order, factor_panels, sizes
    )

    def branch(at):
        return lambda blocks: gather_product(blocks, place, ancestor_inverse, sizes[at], at, size)

    gathered, mine, other = lax.switch(choice[0], [branch(at) for at in range(len(sizes))], packed)
    inverse_panels, sums = finish(
        mine, other, coupling, gathered, live, tree_order, window_at, size
    )
    inverse_diagonal, crosses = close(summed(sums), diag_inverse, coupling, tree_order, size)
    return (inverse_panels, inverse_diagonal, crosses)


def per_device(ancestor_inverse, factor_panels, diag_inverse, coupling, block_pattern, tree_order):
    size = factor_panels.shape[3]
    rows = lax.axis_size("row")
    whole_blocks = math.gcd(ancestor_inverse.shape[1], factor_panels.shape[2]) % size == 0
    paired = rows % 2 == 0 and rows >= 4 and lax.axis_size("col") == 2
    blocks = whole_blocks and size % 128 == 0 and paired and ancestor_inverse.shape[1] <= 1536
    run = per_device_blocks if blocks else per_device_dense
    return run(ancestor_inverse, factor_panels, diag_inverse, coupling, block_pattern, tree_order)


def solution(mesh):
    return jax.shard_map(
        per_device,
        mesh=mesh,
        in_specs=(
            P(None, ("pole", "row"), "col"),
            P(None, None, ("pole", "col", "row"), None),
            P("pole", None, None, None),
            P("pole", None, None, None),
            P(),
            P(),
        ),
        out_specs=(
            P(None, None, ("pole", "row"), None),
            P("pole", None, None, None),
            P("pole", None, None, None),
        ),
        check_vma=False,
    )
```

```python
import functools
import math

import jax
import jax.numpy as jnp
from jax import lax
from jax.experimental import pallas as pl
from jax.experimental.pallas import tpu as pltpu
from jax.sharding import PartitionSpec as P

BF16 = jnp.bfloat16
F32 = jnp.float32
SPARE = 4
VMEM_BYTES = 64 * 1024 * 1024 - 256 * 1024


def swapped(block, axis, bit):
    count = lax.axis_size(axis)
    route = []
    for low in range(count):
        high = low | 1 << bit
        if high != low and high < count:
            route += [(low, high), (high, low)]
    return lax.ppermute(block, axis, route)


def matmul(left_side, right_side):
    return jnp.dot(
        left_side, right_side, preferred_element_type=jnp.float32, precision=lax.Precision.HIGHEST
    )


def multiply(left_side, right_side):
    real_part = matmul(left_side[0], right_side[0]) - matmul(left_side[1], right_side[1])
    imag_part = matmul(left_side[0], right_side[1]) + matmul(left_side[1], right_side[0])
    return jnp.stack([real_part, imag_part])


def flipped(matrix):
    return jnp.swapaxes(matrix, 1, 2)


def row_masks(pattern_eff, first_row, row_count, block_rows):
    row_index = first_row + jnp.arange(row_count, dtype=jnp.int32)
    blocks = row_index // block_rows
    onehot = (blocks[:, None] == jnp.arange(pattern_eff.shape[1], dtype=jnp.int32)[None, :]).astype(
        jnp.float32
    )
    return matmul(pattern_eff, onehot.T)


def per_device_dense(ancestor_inverse, factor_panels, diag_inverse, coupling, block_pattern, tree_order):
    grid_row = lax.axis_index("row")
    grid_col = lax.axis_index("col")
    tile_rows = ancestor_inverse.shape[1]
    half_rows = ancestor_inverse.shape[2]
    piece_rows = factor_panels.shape[2]
    block_rows = factor_panels.shape[3]
    super_count = factor_panels.shape[0]
    share_rows = tile_rows // 2
    sorted_pattern = jnp.take(block_pattern, tree_order, axis=0).astype(jnp.float32)
    pattern_eff = jnp.concatenate(
        [sorted_pattern[:2], sorted_pattern[2:] * sorted_pattern[:2]], axis=0
    )
    source_mask = row_masks(
        pattern_eff, grid_col * half_rows + grid_row * piece_rows, piece_rows, block_rows
    )
    target_mask = row_masks(pattern_eff, grid_row * tile_rows, tile_rows, block_rows)
    panels = jnp.take(factor_panels, tree_order, axis=0) * source_mask[:, None, :, None]
    diag_blocks = jnp.take(diag_inverse, tree_order, axis=0)
    columns = []
    products = []
    for tree_slot in range(super_count):
        gathered = lax.all_gather(panels[tree_slot], "row", axis=1, tiled=True)
        columns.append(gathered)
        products.append(lax.psum(multiply(ancestor_inverse, gathered), "col"))
    own_flag = (grid_row * tile_rows // half_rows == grid_col).astype(jnp.float32)
    offset = jnp.clip(grid_row * tile_rows - grid_col * half_rows, 0, half_rows - tile_rows)
    own_windows = jnp.stack(
        [
            lax.dynamic_slice_in_dim(column_set, offset, tile_rows, 1) * own_flag
            for column_set in columns
        ]
    )
    partner_windows = swapped(own_windows, "col", 0)
    tile_windows = own_windows + partner_windows

    def share(matrix):
        return lax.dynamic_slice_in_dim(matrix, grid_col * share_rows, share_rows, 1)

    windows = [share(tile_windows[tree_slot]) for tree_slot in range(super_count)]
    parent_cols = [
        -target_mask[tree_slot][None, :, None] * products[tree_slot] for tree_slot in range(2)
    ]
    child_cols = [
        -target_mask[tree_slot + 2][None, :, None]
        * (products[tree_slot + 2] + multiply(parent_cols[tree_slot], coupling[tree_slot]))
        for tree_slot in range(2)
    ]
    parent_local = [
        multiply(flipped(windows[tree_slot]), share(parent_cols[tree_slot]))
        for tree_slot in range(2)
    ]
    cross_local = [
        multiply(flipped(share(parent_cols[tree_slot])), windows[tree_slot + 2])
        for tree_slot in range(2)
    ]
    child_local = [
        multiply(flipped(windows[tree_slot + 2]), share(child_cols[tree_slot]))
        for tree_slot in range(2)
    ]
    parent_sums = lax.psum(jnp.stack(parent_local), ("row", "col"))
    parent_diag = [diag_blocks[tree_slot] - parent_sums[tree_slot] for tree_slot in range(2)]
    child_totals = lax.psum(jnp.stack(cross_local + child_local), ("row", "col"))
    crosses = [
        -(child_totals[tree_slot] + multiply(parent_diag[tree_slot], coupling[tree_slot]))
        for tree_slot in range(2)
    ]
    child_sums = [child_totals[2 + tree_slot] for tree_slot in range(2)]
    child_diag = [
        diag_blocks[tree_slot + 2]
        - child_sums[tree_slot]
        - multiply(flipped(coupling[tree_slot]), crosses[tree_slot])
        for tree_slot in range(2)
    ]
    all_cols = jnp.stack(parent_cols + child_cols)
    all_diag = jnp.stack(parent_diag + child_diag)
    inverse_panels = jnp.zeros_like(all_cols).at[tree_order].set(all_cols)
    inverse_diagonal = jnp.zeros_like(all_diag).at[tree_order].set(all_diag)
    return (inverse_panels, inverse_diagonal, jnp.stack(crosses))


def halves(value):
    high = value.astype(BF16)
    return high, (value - high.astype(F32)).astype(BF16)


def prepare_kernel(
    sizes, pattern_ref, order_ref, panels_ref,
    place_ref, window_ref, live_ref, choice_ref, packed_ref,
    held, load_sem, keep_sem,
):
    grid_row, grid_col = lax.axis_index("row"), lax.axis_index("col")
    rows, cols = lax.axis_size("row"), lax.axis_size("col")
    size = panels_ref.shape[3]
    blocks = panels_ref.shape[2] // size
    most = 4 * blocks
    tile_blocks = pattern_ref.shape[1] // rows
    half_blocks = rows * blocks
    order = [order_ref[slot] for slot in range(4)]

    def live_slots(block):
        marks = [pattern_ref[order[slot], block] for slot in range(4)]
        return [
            marks[0] > 0, marks[1] > 0,
            (marks[2] > 0) & (marks[0] > 0), (marks[3] > 0) & (marks[1] > 0),
        ]

    own_start = (grid_col * rows + grid_row) * blocks
    own_live = [live_slots(own_start + block) for block in range(blocks)]

    def load(slot, block, at):
        return pltpu.make_async_copy(
            panels_ref.at[order[slot], :, pl.ds(block * size, size), :], held.at[at], load_sem.at[at]
        )

    at = jnp.int32(0)
    for slot in range(4):
        for block in range(blocks):
            flag = own_live[block][slot]

            @pl.when(flag)
            def _():
                load(slot, block, at).start()

            at = at + flag.astype(jnp.int32)
    own_count = at

    def count_row(row, most_of):
        both = jnp.int32(0)
        largest = most_of[0]
        for half in range(cols):
            total = jnp.int32(0)
            for block in range(blocks):
                for flag in live_slots((half * rows + row) * blocks + block):
                    total = total + flag.astype(jnp.int32)
            largest = jnp.maximum(largest, total)
            both = both + total
        return largest, jnp.maximum(most_of[1], both)

    largest, both = lax.fori_loop(0, rows, count_row, (jnp.int32(0), jnp.int32(0)))
    choice, count = jnp.int32(0), jnp.int32(sizes[0])
    for limit, larger in zip(sizes[:-1], sizes[1:]):
        past = (largest > limit + SPARE) | (both > 2 * limit)
        choice = choice + past.astype(jnp.int32)
        count = jnp.where(past, larger, count)
    choice_ref[0] = choice
    for at_spare in range(SPARE):
        choice_ref[1 + at_spare] = (own_count > count - SPARE + at_spare).astype(jnp.int32)

    def place_piece(piece, _):
        live = [live_slots((grid_col * rows + piece) * blocks + block) for block in range(blocks)]
        spot = jnp.int32(1)
        for slot in range(4):
            for block in range(blocks):
                flag = live[block][slot]
                place_ref[piece * most + slot * blocks + block] = jnp.where(
                    flag, jnp.where(spot > count, 2 * count + SPARE + 1 - spot, spot), 0
                )
                spot = spot + flag.astype(jnp.int32)
        return 0

    lax.fori_loop(0, rows, place_piece, 0)

    def window_row(row, _):
        block = grid_row * tile_blocks + row
        here = (block // half_blocks == grid_col).astype(jnp.int32)
        local = block % half_blocks
        piece, inside = local // blocks, local % blocks
        for slot, flag in enumerate(live_slots(block)):
            live_ref[slot, row] = flag.astype(jnp.int32)
            spot = place_ref[piece * most + slot * blocks + inside]
            window_ref[slot, row] = jnp.where(
                (here > 0) & (spot > 0),
                piece * (most + SPARE) + jnp.where(
                    spot > count, most + spot - count - 1, spot - 1
                ), 0,
            )
        live_ref[4, row] = here
        return 0

    lax.fori_loop(0, tile_blocks, window_row, 0)

    def keep(at):
        return pltpu.make_async_copy(held.at[at], packed_ref.at[at], keep_sem.at[at])

    @pl.loop(0, own_count)
    def _(at):
        load(0, 0, at).wait()
        keep(at).start()

    @pl.loop(0, own_count)
    def _(at):
        keep(at).wait()


def prepare(block_pattern, tree_order, factor_panels, sizes):
    rows = lax.axis_size("row")
    size = factor_panels.shape[3]
    most = 4 * (factor_panels.shape[2] // size)
    tile_blocks = block_pattern.shape[1] // rows
    smem = pl.BlockSpec(memory_space=pltpu.SMEM)
    return pl.pallas_call(
        functools.partial(prepare_kernel, sizes),
        out_shape=(
            jax.ShapeDtypeStruct((rows * most,), jnp.int32),
            jax.ShapeDtypeStruct((4, tile_blocks), jnp.int32),
            jax.ShapeDtypeStruct((5, tile_blocks), jnp.int32),
            jax.ShapeDtypeStruct((1 + SPARE,), jnp.int32),
            jax.ShapeDtypeStruct((most + SPARE, 2, size, size), F32),
        ),
        in_specs=[smem, smem, pl.BlockSpec(memory_space=pl.ANY)],
        out_specs=(smem, smem, smem, smem, pl.BlockSpec(memory_space=pl.ANY)),
        scratch_shapes=[
            pltpu.VMEM((most, 2, size, size), F32),
            pltpu.SemaphoreType.DMA((most,)),
            pltpu.SemaphoreType.DMA((most,)),
        ],
    )(block_pattern, tree_order, factor_panels)


ROW_CHUNK = 256


def part_cuts(count):
    first = max(1, round(count / 8))
    return [0] + [first + (count - first) * at // 3 for at in range(4)]


def relay_plan(lines, count, block_us, unit_us, units):
    cuts = part_cuts(count)
    parts = list(zip(cuts[:-1], cuts[1:]))
    cost = [(high - low) * block_us for low, high in parts]
    beside_time = cost[0]

    def stream(own_items, forwarded):
        clock, landed = 0.0, {}
        for item, ready in own_items + forwarded:
            clock = max(clock, ready) + cost[item[2]]
            landed[item] = clock
        return landed

    climbs = {}
    for way in (1, -1):
        order = range(lines) if way == 1 else range(lines - 1, -1, -1)
        before = {}
        for z in order:
            climbs[way, z] = before
            own = [((z, 0, part), 0.0) for part in (1, 2, 3, 0)] + [((z, 1, 0), beside_time)]
            before = stream(own, sorted(before.items(), key=lambda pair: pair[1]))
    plans = []
    for z in range(lines):
        landed = {**climbs[1, z], **climbs[-1, z]}
        crossing = sorted(
            ((item, when) for item, when in landed.items() if item[1] == 0 and item[2] > 0),
            key=lambda pair: pair[1],
        )
        across = stream([((z, 0, part), 0.0) for part in (0, 1, 2, 3)], crossing)
        ready = {(z, 0): 0.0}
        for item, when in landed.items():
            key = item[:2]
            ready[key] = max(ready.get(key, 0.0), when)
        for item, when in across.items():
            key = (item[0], 1)
            ready[key] = max(ready.get(key, 0.0), when)
        for key in ready:
            ready[key] += 3.0 if key != (z, 0) else 0.0
        events = [((z, 1, 0), beside_time)] + list(landed.items())
        events += [(item[:1] + (1, 3), when) for item, when in across.items() if item[2] == 3]
        events = sorted(events, key=lambda pair: pair[1])
        pieces = sorted(ready, key=lambda key: ready[key])
        clock, at, before_unit, after = 0.0, 0, {}, []
        for turn, piece in enumerate(pieces):
            for unit in range(units):
                start = max(clock, ready[piece]) if unit == 0 else clock
                while at < len(events) and events[at][1] <= start:
                    before_unit.setdefault(turn * units + unit, []).append(events[at][0])
                    at += 1
                clock = start + unit_us
        after = [event for event, _ in events[at:]]
        plans.append((pieces, before_unit, after))
    return parts, plans


def gather_product_kernel(
    rows, parts, plans, size,
    place_ref, choice_ref, own_ref, a_ref, all_ref, mine_ref, other_ref,
    staged, mixed, spare, a_stage, b_high, b_low, acc, mine,
    send_sem, recv_sem, load_sem, keep_sem, a_sem, mine_sem, swap_send, swap_recv,
    lend_send, lend_recv, spare_sem,
):
    here = lax.axis_index("row")
    sibling = 1 - lax.axis_index("col")
    lines = rows // 2
    z, y = here // 2, here % 2
    count = parts[-1][1]
    chunk_rows = a_stage.shape[2]
    chunks = a_ref.shape[1] // chunk_rows
    width = b_high.shape[1]
    blocks = width // size
    beside = z * 2 + (1 - y)
    up, down = here + 2, here - 2
    has_up, has_down = z < lines - 1, z > 0

    most = own_ref.shape[0] - SPARE
    mixed_at = parts[3][0]

    def copy(part, origin, way, target, own=False):
        low, high = parts[part]
        span = pl.ds(low, high - low)
        source = mixed if part == 3 else own_ref.at[span]
        return pltpu.make_async_remote_copy(
            src_ref=source if own else all_ref.at[origin, span],
            dst_ref=all_ref.at[origin, span],
            send_sem=send_sem.at[part, origin, way],
            recv_sem=recv_sem.at[part, origin],
            device_id={"row": target},
            device_id_type=pl.DeviceIdType.MESH,
        )

    def lend(origin):
        return pltpu.make_async_remote_copy(
            src_ref=all_ref.at[origin, pl.ds(count - SPARE, SPARE)],
            dst_ref=all_ref.at[origin, pl.ds(most, SPARE)],
            send_sem=lend_send.at[origin],
            recv_sem=lend_recv.at[origin],
            device_id={"col": sibling},
            device_id_type=pl.DeviceIdType.MESH,
        )

    def arrived(part, origin):
        copy(part, origin, 0, beside).wait_recv()

    barrier = pltpu.get_barrier_semaphore()

    def greet(target):
        pl.semaphore_signal(barrier, inc=1, device_id=target, device_id_type=pl.DeviceIdType.MESH)

    greet({"row": beside})
    greet({"col": sibling})

    @pl.when(has_up)
    def _():
        greet({"row": up})

    @pl.when(has_down)
    def _():
        greet({"row": down})

    pl.semaphore_wait(barrier, 2 + has_up.astype(jnp.int32) + has_down.astype(jnp.int32))

    spare_copy = pltpu.make_async_remote_copy(
        src_ref=own_ref.at[pl.ds(count, SPARE)],
        dst_ref=spare,
        send_sem=spare_sem.at[0],
        recv_sem=spare_sem.at[1],
        device_id={"col": sibling},
        device_id_type=pl.DeviceIdType.MESH,
    )
    spare_copy.start()
    mixed_copy = pltpu.make_async_copy(
        own_ref.at[pl.ds(mixed_at, count - mixed_at)], mixed, keep_sem
    )
    mixed_copy.start()

    def send_own(part):
        @pl.when(has_up)
        def _():
            copy(part, here, 0, up, True).start()

        @pl.when(has_down)
        def _():
            copy(part, here, 1, down, True).start()

        if part:
            copy(part, here, 2, beside, True).start()

    copy(0, here, 2, beside, True).start()
    send_own(1)
    send_own(2)
    own_loads = [
        pltpu.make_async_copy(own_ref.at[pl.ds(0, count)], staged.at[pl.ds(1, count)], load_sem.at[0])
    ] + [
        pltpu.make_async_copy(
            own_ref.at[count + at], staged.at[count + SPARE - at], load_sem.at[1 + at]
        )
        for at in range(SPARE)
    ]
    for load in own_loads:
        load.start()
    mixed_copy.wait()
    spare_copy.wait()
    for at in range(SPARE):
        target = count - SPARE + at - mixed_at
        mixed[target] = jnp.where(choice_ref[1 + at] > 0, mixed[target], spare[SPARE - 1 - at])
    for load in own_loads:
        load.wait()
    send_own(3)
    send_own(0)

    def origin_of(turn):
        origin = here
        for line, (pieces, _, _) in enumerate(plans):
            for at, (from_line, side) in enumerate(pieces):
                origin = jnp.where(
                    (z == line) & (turn == at), from_line * 2 + (y if side == 0 else 1 - y), origin
                )
        return origin

    def a_copy(step, origin):
        chunk = step % chunks
        return pltpu.make_async_copy(
            a_ref.at[
                :,
                pl.ds(pl.multiple_of(chunk * chunk_rows, 8), chunk_rows),
                pl.ds(pl.multiple_of(origin * width, 128), width),
            ],
            a_stage.at[step % 2],
            a_sem.at[step % 2],
        )

    a_copy(0, origin_of(0)).start()
    a_copy(1, origin_of(1 // chunks)).start()
    acc[...] = jnp.zeros_like(acc)
    staged[0] = jnp.zeros(staged.shape[1:], F32)

    def relay(line, item):
        from_line, side, part = item
        origin = from_line * 2 + (y if side == 0 else 1 - y)
        arrived(part, origin)
        if part == 3:
            lend(origin).start()
        if side == 1 and part:
            return
        if from_line == line:
            ways = ([0] if line < lines - 1 else []) + ([1] if line > 0 else [])
        elif from_line < line:
            ways = [0] if line < lines - 1 else []
        else:
            ways = [1] if line > 0 else []
        for way in ways:
            copy(part, origin, way, up if way == 0 else down).start()
        if side == 0 and part:
            copy(part, origin, 2, beside).start()

    def a_step(step, _):
        turn, chunk = step // chunks, step % chunks
        for line, (pieces, before_unit, _) in enumerate(plans):
            @pl.when(z == line)
            def _():
                for at in sorted(before_unit):
                    @pl.when(step == at)
                    def _():
                        for item in before_unit[at]:
                            relay(line, item)

        @pl.when(chunk == 0)
        def _():
            for line, (pieces, _, _) in enumerate(plans):
                for at, (from_line, side) in enumerate(pieces):
                    if side == 1:
                        @pl.when((z == line) & (turn == at))
                        def _():
                            for part in (1, 2):
                                arrived(part, from_line * 2 + (1 - y))

            origin = origin_of(turn)

            def keeps():
                return [
                    pltpu.make_async_copy(
                        staged.at[pl.ds(1, count)], all_ref.at[here, pl.ds(0, count)], keep_sem
                    ),
                    pltpu.make_async_copy(
                        staged.at[pl.ds(1 + count, SPARE)], all_ref.at[here, pl.ds(most, SPARE)],
                        load_sem.at[1],
                    ),
                ]

            @pl.when(turn == 0)
            def _():
                for keep in keeps():
                    keep.start()

            @pl.when(turn == 1)
            def _():
                for keep in keeps():
                    keep.wait()

            @pl.when(turn > 0)
            def _():
                load = pltpu.make_async_copy(
                    all_ref.at[origin, pl.ds(0, count)], staged.at[pl.ds(1, count)], load_sem.at[0]
                )
                load.start()
                lend(origin).wait_recv()
                lent = pltpu.make_async_copy(
                    all_ref.at[origin, pl.ds(most, SPARE)], staged.at[pl.ds(1 + count, SPARE)],
                    load_sem.at[1],
                )
                lent.start()
                load.wait()
                lent.wait()

            def spread(block, _):
                span = pl.ds(pl.multiple_of(block * size, size), size)
                for slot in range(4):
                    value = staged[place_ref[origin * (4 * blocks) + slot * blocks + block]]
                    for kind, term in enumerate((value[0], value[1], value[0] + value[1])):
                        high, low = halves(term)
                        b_high[kind, span, slot * size:(slot + 1) * size] = high
                        b_low[kind, span, slot * size:(slot + 1) * size] = low
                return 0

            lax.fori_loop(0, blocks, spread, 0)

        a_copy(step, here).wait()
        span = pl.ds(pl.multiple_of(chunk * chunk_rows, 8), chunk_rows)
        real, imag = a_stage[step % 2, 0], a_stage[step % 2, 1]
        for kind, term in enumerate((real, imag, real + imag)):
            high, low = halves(term)
            acc[kind, span, :] += jnp.dot(
                jnp.concatenate([high, low, high], axis=1),
                jnp.concatenate([b_high[kind], b_high[kind], b_low[kind]], axis=0),
                preferred_element_type=F32,
            )

        @pl.when(step + 2 < rows * chunks)
        def _():
            a_copy(step + 2, origin_of((step + 2) // chunks)).start()

        @pl.when(turn == rows - 1)
        def _():
            for slot in range(4):
                columns = slice(slot * size, (slot + 1) * size)
                first, second = acc[0, span, columns], acc[1, span, columns]
                mine[slot, 0, span] = first - second
                mine[slot, 1, span] = acc[2, span, columns] - first - second
            swap(chunk).start()
            keep_mine(chunk).start()

        return 0

    def swap(chunk):
        span = pl.ds(pl.multiple_of(chunk * chunk_rows, 8), chunk_rows)
        return pltpu.make_async_remote_copy(
            src_ref=mine.at[:, :, span],
            dst_ref=other_ref.at[:, :, span],
            send_sem=swap_send.at[chunk],
            recv_sem=swap_recv.at[chunk],
            device_id={"col": sibling},
            device_id_type=pl.DeviceIdType.MESH,
        )

    def keep_mine(chunk):
        span = pl.ds(pl.multiple_of(chunk * chunk_rows, 8), chunk_rows)
        return pltpu.make_async_copy(mine.at[:, :, span], mine_ref.at[:, :, span], mine_sem.at[chunk])

    lax.fori_loop(0, rows * chunks, a_step, 0)

    for line, (_, _, after) in enumerate(plans):
        if after:
            @pl.when(z == line)
            def _():
                for item in after:
                    relay(line, item)

    for chunk in range(chunks):
        swap(chunk).wait()
        keep_mine(chunk).wait()

    copy(0, here, 2, beside, True).wait_send()
    for line in range(lines):
        lend(line * 2 + (1 - y)).wait_send()

        @pl.when(z != line)
        def _():
            lend(line * 2 + y).wait_send()

        for part in (1, 2, 3):
            copy(part, line * 2 + y, 2, beside).wait_send()
        for part, origin in [(part, line * 2 + y) for part in (1, 2, 3, 0)] + [(0, line * 2 + 1 - y)]:
            @pl.when(has_up & (line <= z))
            def _():
                copy(part, origin, 0, up).wait_send()

            @pl.when(has_down & (line >= z))
            def _():
                copy(part, origin, 1, down).wait_send()


def gather_product(packed, place, choice, ancestor_inverse, count, branch, size):
    rows = lax.axis_size("row")
    tile_rows, half_rows = ancestor_inverse.shape[1:]
    width = half_rows // rows
    chunk_rows = math.gcd(tile_rows, ROW_CHUNK)
    chunks = tile_rows // chunk_rows
    parts, plans = relay_plan(rows // 2, count, 2.82, 16.0 / chunks, chunks)
    column_shape = jax.ShapeDtypeStruct((4, 2, tile_rows, size), F32)
    return pl.pallas_call(
        functools.partial(gather_product_kernel, rows, parts, plans, size),
        out_shape=(
            jax.ShapeDtypeStruct((rows,) + packed.shape, F32), column_shape, column_shape,
        ),
        in_specs=[
            pl.BlockSpec(memory_space=pltpu.SMEM),
            pl.BlockSpec(memory_space=pltpu.SMEM),
            pl.BlockSpec(memory_space=pl.ANY),
            pl.BlockSpec(memory_space=pl.ANY),
        ],
        out_specs=(pl.BlockSpec(memory_space=pl.ANY),) * 3,
        scratch_shapes=[
            pltpu.VMEM((count + 1 + SPARE,) + packed.shape[1:], F32),
            pltpu.VMEM((count - parts[3][0],) + packed.shape[1:], F32),
            pltpu.VMEM((SPARE,) + packed.shape[1:], F32),
            pltpu.VMEM((2, 2, chunk_rows, width), F32),
            pltpu.VMEM((3, width, 4 * size), BF16),
            pltpu.VMEM((3, width, 4 * size), BF16),
            pltpu.VMEM((3, tile_rows, 4 * size), F32),
            pltpu.VMEM((4, 2, tile_rows, size), F32),
            pltpu.SemaphoreType.DMA((4, rows, 3)),
            pltpu.SemaphoreType.DMA((4, rows)),
            pltpu.SemaphoreType.DMA((1 + SPARE,)),
            pltpu.SemaphoreType.DMA,
            pltpu.SemaphoreType.DMA((2,)),
            pltpu.SemaphoreType.DMA((chunks,)),
            pltpu.SemaphoreType.DMA((chunks,)),
            pltpu.SemaphoreType.DMA((chunks,)),
            pltpu.SemaphoreType.DMA((rows,)),
            pltpu.SemaphoreType.DMA((rows,)),
            pltpu.SemaphoreType.DMA((2,)),
        ],
        compiler_params=pltpu.CompilerParams(
            collective_id=branch + 1, has_side_effects=True, vmem_limit_bytes=VMEM_BYTES
        ),
    )(place, choice, packed, ancestor_inverse)


def wide(matrix):
    return jnp.concatenate([matrix[0], matrix[1]], axis=1)


def folded(product, size):
    return jnp.stack(
        [
            product[:size, :size] - product[size:, size:],
            product[:size, size:] + product[size:, :size],
        ]
    )


def contracted(left_side, right_side):
    return lax.dot_general(
        left_side, right_side, (((0,), (0,)), ((), ())), preferred_element_type=F32
    )


def tripled(value, axis, right):
    high, low = halves(value)
    return jnp.concatenate([high, high, low] if right else [high, low, high], axis=axis)


def finish_kernel(
    size, live_ref, order_ref, window_at_ref,
    mine_ref, other_ref, link_ref, w0_ref, w1_ref, w2_ref, w3_ref,
    columns_ref, sums_ref, acc,
):
    row = pl.program_id(0)
    windows = (w0_ref, w1_ref, w2_ref, w3_ref)

    @pl.when(row == 0)
    def _():
        acc[...] = jnp.zeros_like(acc)

    for tree in range(2):
        child = tree + 2
        parent_at = order_ref[tree]
        child_at = order_ref[child]

        @pl.when(live_ref[tree, row] == 0)
        def _():
            columns_ref[parent_at] = jnp.zeros(columns_ref.shape[1:], F32)

        @pl.when(live_ref[child, row] == 0)
        def _():
            columns_ref[child_at] = jnp.zeros(columns_ref.shape[1:], F32)

        @pl.when(live_ref[tree, row] > 0)
        def _():
            columns_ref[parent_at] = -(mine_ref[tree] + other_ref[tree])

        @pl.when(live_ref[child, row] > 0)
        def _():
            parent = columns_ref[parent_at]
            linked = jnp.dot(
                tripled(jnp.concatenate([parent[0], parent[1]], axis=0), 1, False),
                tripled(wide(link_ref[tree]), 0, True),
                preferred_element_type=F32,
            )
            columns_ref[child_at] = -(mine_ref[child] + other_ref[child] + folded(linked, size))

        @pl.when((live_ref[4, row] > 0) & (live_ref[tree, row] > 0))
        def _():
            parent = tripled(wide(columns_ref[parent_at]), 0, True)

            @pl.when(live_ref[child, row] == 0)
            def _():
                acc[tree, :2 * size, :2 * size] += contracted(
                    tripled(wide(windows[tree][0]), 0, False), parent
                )

            @pl.when(live_ref[child, row] > 0)
            def _():
                acc[tree] += contracted(
                    jnp.concatenate(
                        [tripled(wide(windows[at][0]), 0, False) for at in (tree, child)], axis=1
                    ),
                    jnp.concatenate(
                        [parent, tripled(wide(columns_ref[child_at]), 0, True)], axis=1
                    ),
                )

    @pl.when(row == pl.num_programs(0) - 1)
    def _():
        for tree in range(2):
            for kind, (high, wide_at) in enumerate(((0, 0), (1, 0), (1, 1))):
                block = acc[
                    tree, 2 * size * high:2 * size * (high + 1),
                    2 * size * wide_at:2 * size * (wide_at + 1),
                ]
                sums_ref[2 * kind + tree] = folded(block, size)


def finish(mine, other, coupling, gathered, live, tree_order, window_at, size):
    rows = live.shape[1]
    gathered = gathered.reshape((-1,) + gathered.shape[2:])

    def window_map(slot, g, live, order, window_at):
        return (window_at[slot, g], 0, 0, 0)

    return pl.pallas_call(
        functools.partial(finish_kernel, size),
        out_shape=(
            jax.ShapeDtypeStruct(mine.shape, F32),
            jax.ShapeDtypeStruct((6, 2, size, size), F32),
        ),
        grid_spec=pltpu.PrefetchScalarGridSpec(
            num_scalar_prefetch=3,
            grid=(rows,),
            in_specs=[
                pl.BlockSpec((4, 2, size, size), lambda g, *_: (0, 0, g, 0)),
                pl.BlockSpec((4, 2, size, size), lambda g, *_: (0, 0, g, 0)),
                pl.BlockSpec(coupling.shape, lambda g, *_: (0, 0, 0, 0)),
            ]
            + [
                pl.BlockSpec((1, 2, size, size), functools.partial(window_map, slot))
                for slot in range(4)
            ],
            out_specs=(
                pl.BlockSpec((4, 2, size, size), lambda g, *_: (0, 0, g, 0)),
                pl.BlockSpec((6, 2, size, size), lambda g, *_: (0, 0, 0, 0)),
            ),
            scratch_shapes=[pltpu.VMEM((2, 4 * size, 4 * size), F32)],
        ),
        compiler_params=pltpu.CompilerParams(vmem_limit_bytes=VMEM_BYTES),
    )(live, tree_order, window_at, mine, other, coupling, gathered, gathered, gathered, gathered)


def close_kernel(size, order_ref, totals_ref, diag_ref, link_ref, diagonal_ref, cross_ref):
    def times(left_side, right_side):
        return folded(
            matmul(jnp.concatenate([left_side[0], left_side[1]], axis=0), wide(right_side)), size
        )

    for tree in range(2):
        parent_at, child_at = order_ref[tree], order_ref[tree + 2]
        link = link_ref[tree]
        parent = diag_ref[parent_at] - totals_ref[tree]
        crossed = jnp.stack([totals_ref[2 + tree, part].T for part in range(2)])
        cross = -(crossed + times(parent, link))
        turned = jnp.stack([link[part].T for part in range(2)])
        diagonal_ref[parent_at] = parent
        cross_ref[tree] = cross
        diagonal_ref[child_at] = diag_ref[child_at] - totals_ref[4 + tree] - times(turned, cross)


def close(totals, diag_inverse, coupling, tree_order, size):
    whole = pl.BlockSpec(memory_space=pltpu.VMEM)
    return pl.pallas_call(
        functools.partial(close_kernel, size),
        out_shape=(
            jax.ShapeDtypeStruct(diag_inverse.shape, F32),
            jax.ShapeDtypeStruct(coupling.shape, F32),
        ),
        in_specs=[pl.BlockSpec(memory_space=pltpu.SMEM), whole, whole, whole],
        out_specs=(whole, whole),
    )(tree_order, totals, diag_inverse, coupling)


def sum_kernel(routes, part_ref, sum_ref, total, landed, send_sem, recv_sem):
    barrier = pltpu.get_barrier_semaphore()

    def partner_of(axis, bit):
        at = lax.axis_index(axis)
        mine = (at // (1 << bit)) % 2
        return at + (1 << bit) * (1 - 2 * mine), mine

    for axis, bit in routes[0]:
        pl.semaphore_signal(
            barrier, inc=1, device_id={axis: partner_of(axis, bit)[0]},
            device_id_type=pl.DeviceIdType.MESH,
        )
    pl.semaphore_wait(barrier, len(routes[0]))

    def copy(route, stage, source, source_at, target, target_at, length):
        axis, bit = routes[route][stage % len(routes[route])]
        return pltpu.make_async_remote_copy(
            src_ref=source.at[pl.ds(source_at, length)],
            dst_ref=target.at[pl.ds(target_at, length)],
            send_sem=send_sem.at[route, stage],
            recv_sem=recv_sem.at[route, stage],
            device_id={axis: partner_of(axis, bit)[0]},
            device_id_type=pl.DeviceIdType.MESH,
        )

    total[...] = part_ref[...]
    stages = len(routes[0])
    whole = part_ref.shape[0] // len(routes)
    length = whole
    starts = [whole * route for route in range(len(routes))]
    landings = list(starts)
    spans = []
    for stage in range(stages):
        length = length // 2
        copies, keeps = [], []
        for route in range(len(routes)):
            mine = partner_of(*routes[route][stage])[1]
            keep = pl.multiple_of(starts[route] + mine * length, 8)
            give = pl.multiple_of(starts[route] + (1 - mine) * length, 8)
            move = copy(route, stage, total, give, landed, landings[route], length)
            move.start()
            copies.append(move)
            keeps.append(keep)
        for route in range(len(routes)):
            copies[route].wait()
            landing = landings[route]
            total[pl.ds(keeps[route], length)] += landed[pl.ds(landing, length)]
            landings[route] = landing + length
        starts = keeps
        spans.append((keeps, length))
    for route in range(len(routes)):
        sum_ref[pl.ds(starts[route], length)] = total[pl.ds(starts[route], length)]
    for stage in reversed(range(stages)):
        keeps, length = spans[stage]
        copies = []
        for route in range(len(routes)):
            keep = keeps[route]
            move = copy(route, stages + stage, sum_ref, keep, sum_ref, keep, length)
            move.start()
            copies.append(move)
        for move in copies:
            move.wait()


def summed(parts):
    stages = []
    for axis in ("col", "row"):
        count = lax.axis_size(axis)
        if count & (count - 1):
            return lax.psum(parts, ("row", "col"))
        stages += [(axis, bit) for bit in range(count.bit_length() - 1)]
    flat = parts.reshape(-1, parts.shape[-1])
    if flat.shape[0] % (16 << len(stages)) or len(stages) < 3:
        return lax.psum(parts, ("row", "col"))
    routes = (tuple(stages), (stages[0], *stages[2:], stages[1]))
    total = pl.pallas_call(
        functools.partial(sum_kernel, routes),
        out_shape=jax.ShapeDtypeStruct(flat.shape, F32),
        in_specs=[pl.BlockSpec(memory_space=pltpu.VMEM)],
        out_specs=pl.BlockSpec(memory_space=pltpu.VMEM),
        scratch_shapes=[
            pltpu.VMEM(flat.shape, F32),
            pltpu.VMEM(flat.shape, F32),
            pltpu.SemaphoreType.DMA((2, 2 * len(stages))),
            pltpu.SemaphoreType.DMA((2, 2 * len(stages))),
        ],
        compiler_params=pltpu.CompilerParams(collective_id=0, has_side_effects=True),
    )(flat)
    return total.reshape(parts.shape)


def per_device_blocks(
    ancestor_inverse, factor_panels, diag_inverse, coupling, block_pattern, tree_order
):
    size = factor_panels.shape[3]
    most = 4 * (factor_panels.shape[2] // size)
    least = (most + 1) // 2
    sizes = sorted({*range(least + 2, min(least + 7, most)), least + (most - least) * 2 // 3, most})
    sizes = [size_of for size_of in sizes if size_of - part_cuts(size_of)[3] >= SPARE]
    place, window_at, live, choice, packed = prepare(
        block_pattern, tree_order, factor_panels, sizes
    )

    def branch(at):
        return lambda blocks: gather_product(
            blocks, place, choice, ancestor_inverse, sizes[at], at, size
        )

    gathered, mine, other = lax.switch(choice[0], [branch(at) for at in range(len(sizes))], packed)
    inverse_panels, sums = finish(
        mine, other, coupling, gathered, live, tree_order, window_at, size
    )
    inverse_diagonal, crosses = close(summed(sums), diag_inverse, coupling, tree_order, size)
    return (inverse_panels, inverse_diagonal, crosses)


def per_device(ancestor_inverse, factor_panels, diag_inverse, coupling, block_pattern, tree_order):
    size = factor_panels.shape[3]
    rows = lax.axis_size("row")
    whole_blocks = math.gcd(ancestor_inverse.shape[1], factor_panels.shape[2]) % size == 0
    paired = rows % 2 == 0 and rows >= 4 and lax.axis_size("col") == 2
    blocks = whole_blocks and size % 128 == 0 and paired and ancestor_inverse.shape[1] <= 1536
    run = per_device_blocks if blocks else per_device_dense
    return run(ancestor_inverse, factor_panels, diag_inverse, coupling, block_pattern, tree_order)


def solution(mesh):
    return jax.shard_map(
        per_device,
        mesh=mesh,
        in_specs=(
            P(None, ("pole", "row"), "col"),
            P(None, None, ("pole", "col", "row"), None),
            P("pole", None, None, None),
            P("pole", None, None, None),
            P(),
            P(),
        ),
        out_specs=(
            P(None, None, ("pole", "row"), None),
            P("pole", None, None, None),
            P("pole", None, None, None),
        ),
        check_vma=False,
    )
```

```python
import functools
import math

import jax
import jax.numpy as jnp
from jax import lax
from jax.experimental import pallas as pl
from jax.experimental.pallas import tpu as pltpu
from jax.sharding import PartitionSpec as P

BF16 = jnp.bfloat16
F32 = jnp.float32
SPARE = 4
VMEM_BYTES = 64 * 1024 * 1024 - 256 * 1024


def swapped(block, axis, bit):
    count = lax.axis_size(axis)
    route = []
    for low in range(count):
        high = low | 1 << bit
        if high != low and high < count:
            route += [(low, high), (high, low)]
    return lax.ppermute(block, axis, route)


def matmul(left_side, right_side):
    return jnp.dot(
        left_side, right_side, preferred_element_type=jnp.float32, precision=lax.Precision.HIGHEST
    )


def multiply(left_side, right_side):
    real_part = matmul(left_side[0], right_side[0]) - matmul(left_side[1], right_side[1])
    imag_part = matmul(left_side[0], right_side[1]) + matmul(left_side[1], right_side[0])
    return jnp.stack([real_part, imag_part])


def flipped(matrix):
    return jnp.swapaxes(matrix, 1, 2)


def row_masks(pattern_eff, first_row, row_count, block_rows):
    row_index = first_row + jnp.arange(row_count, dtype=jnp.int32)
    blocks = row_index // block_rows
    onehot = (blocks[:, None] == jnp.arange(pattern_eff.shape[1], dtype=jnp.int32)[None, :]).astype(
        jnp.float32
    )
    return matmul(pattern_eff, onehot.T)


def per_device_dense(ancestor_inverse, factor_panels, diag_inverse, coupling, block_pattern, tree_order):
    grid_row = lax.axis_index("row")
    grid_col = lax.axis_index("col")
    tile_rows = ancestor_inverse.shape[1]
    half_rows = ancestor_inverse.shape[2]
    piece_rows = factor_panels.shape[2]
    block_rows = factor_panels.shape[3]
    super_count = factor_panels.shape[0]
    share_rows = tile_rows // 2
    sorted_pattern = jnp.take(block_pattern, tree_order, axis=0).astype(jnp.float32)
    pattern_eff = jnp.concatenate(
        [sorted_pattern[:2], sorted_pattern[2:] * sorted_pattern[:2]], axis=0
    )
    source_mask = row_masks(
        pattern_eff, grid_col * half_rows + grid_row * piece_rows, piece_rows, block_rows
    )
    target_mask = row_masks(pattern_eff, grid_row * tile_rows, tile_rows, block_rows)
    panels = jnp.take(factor_panels, tree_order, axis=0) * source_mask[:, None, :, None]
    diag_blocks = jnp.take(diag_inverse, tree_order, axis=0)
    columns = []
    products = []
    for tree_slot in range(super_count):
        gathered = lax.all_gather(panels[tree_slot], "row", axis=1, tiled=True)
        columns.append(gathered)
        products.append(lax.psum(multiply(ancestor_inverse, gathered), "col"))
    own_flag = (grid_row * tile_rows // half_rows == grid_col).astype(jnp.float32)
    offset = jnp.clip(grid_row * tile_rows - grid_col * half_rows, 0, half_rows - tile_rows)
    own_windows = jnp.stack(
        [
            lax.dynamic_slice_in_dim(column_set, offset, tile_rows, 1) * own_flag
            for column_set in columns
        ]
    )
    partner_windows = swapped(own_windows, "col", 0)
    tile_windows = own_windows + partner_windows

    def share(matrix):
        return lax.dynamic_slice_in_dim(matrix, grid_col * share_rows, share_rows, 1)

    windows = [share(tile_windows[tree_slot]) for tree_slot in range(super_count)]
    parent_cols = [
        -target_mask[tree_slot][None, :, None] * products[tree_slot] for tree_slot in range(2)
    ]
    child_cols = [
        -target_mask[tree_slot + 2][None, :, None]
        * (products[tree_slot + 2] + multiply(parent_cols[tree_slot], coupling[tree_slot]))
        for tree_slot in range(2)
    ]
    parent_local = [
        multiply(flipped(windows[tree_slot]), share(parent_cols[tree_slot]))
        for tree_slot in range(2)
    ]
    cross_local = [
        multiply(flipped(share(parent_cols[tree_slot])), windows[tree_slot + 2])
        for tree_slot in range(2)
    ]
    child_local = [
        multiply(flipped(windows[tree_slot + 2]), share(child_cols[tree_slot]))
        for tree_slot in range(2)
    ]
    parent_sums = lax.psum(jnp.stack(parent_local), ("row", "col"))
    parent_diag = [diag_blocks[tree_slot] - parent_sums[tree_slot] for tree_slot in range(2)]
    child_totals = lax.psum(jnp.stack(cross_local + child_local), ("row", "col"))
    crosses = [
        -(child_totals[tree_slot] + multiply(parent_diag[tree_slot], coupling[tree_slot]))
        for tree_slot in range(2)
    ]
    child_sums = [child_totals[2 + tree_slot] for tree_slot in range(2)]
    child_diag = [
        diag_blocks[tree_slot + 2]
        - child_sums[tree_slot]
        - multiply(flipped(coupling[tree_slot]), crosses[tree_slot])
        for tree_slot in range(2)
    ]
    all_cols = jnp.stack(parent_cols + child_cols)
    all_diag = jnp.stack(parent_diag + child_diag)
    inverse_panels = jnp.zeros_like(all_cols).at[tree_order].set(all_cols)
    inverse_diagonal = jnp.zeros_like(all_diag).at[tree_order].set(all_diag)
    return (inverse_panels, inverse_diagonal, jnp.stack(crosses))


def halves(value):
    high = value.astype(BF16)
    return high, (value - high.astype(F32)).astype(BF16)


def prepare_kernel(
    sizes, pattern_ref, order_ref, panels_ref,
    place_ref, window_ref, live_ref, choice_ref, packed_ref,
    held, load_sem, keep_sem,
):
    grid_row, grid_col = lax.axis_index("row"), lax.axis_index("col")
    rows, cols = lax.axis_size("row"), lax.axis_size("col")
    size = panels_ref.shape[3]
    blocks = panels_ref.shape[2] // size
    most = 4 * blocks
    tile_blocks = pattern_ref.shape[1] // rows
    half_blocks = rows * blocks
    order = [order_ref[slot] for slot in range(4)]

    def live_slots(block):
        marks = [pattern_ref[order[slot], block] for slot in range(4)]
        return [
            marks[0] > 0, marks[1] > 0,
            (marks[2] > 0) & (marks[0] > 0), (marks[3] > 0) & (marks[1] > 0),
        ]

    own_start = (grid_col * rows + grid_row) * blocks
    own_live = [live_slots(own_start + block) for block in range(blocks)]

    def load(slot, block, at):
        return pltpu.make_async_copy(
            panels_ref.at[order[slot], :, pl.ds(block * size, size), :], held.at[at], load_sem.at[at]
        )

    at = jnp.int32(0)
    for slot in range(4):
        for block in range(blocks):
            flag = own_live[block][slot]

            @pl.when(flag)
            def _():
                load(slot, block, at).start()

            at = at + flag.astype(jnp.int32)
    own_count = at

    def count_row(row, most_of):
        both = jnp.int32(0)
        largest = most_of[0]
        for half in range(cols):
            total = jnp.int32(0)
            for block in range(blocks):
                for flag in live_slots((half * rows + row) * blocks + block):
                    total = total + flag.astype(jnp.int32)
            largest = jnp.maximum(largest, total)
            both = both + total
        return largest, jnp.maximum(most_of[1], both)

    largest, both = lax.fori_loop(0, rows, count_row, (jnp.int32(0), jnp.int32(0)))
    choice, count = jnp.int32(0), jnp.int32(sizes[0])
    for limit, larger in zip(sizes[:-1], sizes[1:]):
        past = (largest > limit + SPARE) | (both > 2 * limit)
        choice = choice + past.astype(jnp.int32)
        count = jnp.where(past, larger, count)
    choice_ref[0] = choice
    for at_spare in range(SPARE):
        choice_ref[1 + at_spare] = (own_count > count - SPARE + at_spare).astype(jnp.int32)

    def place_piece(piece, _):
        live = [live_slots((grid_col * rows + piece) * blocks + block) for block in range(blocks)]
        spot = jnp.int32(1)
        for slot in range(4):
            for block in range(blocks):
                flag = live[block][slot]
                place_ref[piece * most + slot * blocks + block] = jnp.where(
                    flag, jnp.where(spot > count, 2 * count + SPARE + 1 - spot, spot), 0
                )
                spot = spot + flag.astype(jnp.int32)
        return 0

    lax.fori_loop(0, rows, place_piece, 0)

    def window_row(row, _):
        block = grid_row * tile_blocks + row
        here = (block // half_blocks == grid_col).astype(jnp.int32)
        local = block % half_blocks
        piece, inside = local // blocks, local % blocks
        for slot, flag in enumerate(live_slots(block)):
            live_ref[slot, row] = flag.astype(jnp.int32)
            spot = place_ref[piece * most + slot * blocks + inside]
            window_ref[slot, row] = jnp.where(
                (here > 0) & (spot > 0),
                piece * (most + SPARE) + jnp.where(
                    spot > count, most + spot - count - 1, spot - 1
                ), 0,
            )
        live_ref[4, row] = here
        return 0

    lax.fori_loop(0, tile_blocks, window_row, 0)

    def keep(at):
        return pltpu.make_async_copy(held.at[at], packed_ref.at[at], keep_sem.at[at])

    @pl.loop(0, own_count)
    def _(at):
        load(0, 0, at).wait()
        keep(at).start()

    @pl.loop(0, own_count)
    def _(at):
        keep(at).wait()


def prepare(block_pattern, tree_order, factor_panels, sizes):
    rows = lax.axis_size("row")
    size = factor_panels.shape[3]
    most = 4 * (factor_panels.shape[2] // size)
    tile_blocks = block_pattern.shape[1] // rows
    smem = pl.BlockSpec(memory_space=pltpu.SMEM)
    return pl.pallas_call(
        functools.partial(prepare_kernel, sizes),
        out_shape=(
            jax.ShapeDtypeStruct((rows * most,), jnp.int32),
            jax.ShapeDtypeStruct((4, tile_blocks), jnp.int32),
            jax.ShapeDtypeStruct((5, tile_blocks), jnp.int32),
            jax.ShapeDtypeStruct((1 + SPARE,), jnp.int32),
            jax.ShapeDtypeStruct((most + SPARE, 2, size, size), F32),
        ),
        in_specs=[smem, smem, pl.BlockSpec(memory_space=pl.ANY)],
        out_specs=(smem, smem, smem, smem, pl.BlockSpec(memory_space=pl.ANY)),
        scratch_shapes=[
            pltpu.VMEM((most, 2, size, size), F32),
            pltpu.SemaphoreType.DMA((most,)),
            pltpu.SemaphoreType.DMA((most,)),
        ],
    )(block_pattern, tree_order, factor_panels)


ROW_CHUNK = 256


def part_cuts(count):
    first = max(1, round(count / 8))
    return [0] + [first + (count - first) * at // 3 for at in range(4)]


def relay_plan(lines, count, block_us, unit_us, units):
    cuts = part_cuts(count)
    parts = list(zip(cuts[:-1], cuts[1:]))
    cost = [(high - low) * block_us for low, high in parts]
    beside_time = cost[0]

    def stream(own_items, forwarded):
        clock, landed = 0.0, {}
        for item, ready in own_items + forwarded:
            clock = max(clock, ready) + cost[item[2]]
            landed[item] = clock
        return landed

    climbs = {}
    for way in (1, -1):
        order = range(lines) if way == 1 else range(lines - 1, -1, -1)
        before = {}
        for z in order:
            climbs[way, z] = before
            own = [((z, 0, part), 0.0) for part in (1, 2, 3, 0)] + [((z, 1, 0), beside_time)]
            before = stream(own, sorted(before.items(), key=lambda pair: pair[1]))
    plans = []
    for z in range(lines):
        landed = {**climbs[1, z], **climbs[-1, z]}
        crossing = sorted(
            ((item, when) for item, when in landed.items() if item[1] == 0 and item[2] > 0),
            key=lambda pair: pair[1],
        )
        across = stream([((z, 0, part), 0.0) for part in (0, 1, 2, 3)], crossing)
        ready = {(z, 0): 0.0}
        for item, when in landed.items():
            key = item[:2]
            ready[key] = max(ready.get(key, 0.0), when)
        for item, when in across.items():
            key = (item[0], 1)
            ready[key] = max(ready.get(key, 0.0), when)
        for key in ready:
            ready[key] += 3.0 if key != (z, 0) else 0.0
        events = [((z, 1, 0), beside_time)] + list(landed.items())
        events += [(item[:1] + (1, 3), when) for item, when in across.items() if item[2] == 3]
        events = sorted(events, key=lambda pair: pair[1])
        pieces = sorted(ready, key=lambda key: ready[key])
        clock, at, before_unit, after = 0.0, 0, {}, []
        for turn, piece in enumerate(pieces):
            for unit in range(units):
                start = max(clock, ready[piece]) if unit == 0 else clock
                while at < len(events) and events[at][1] <= start:
                    before_unit.setdefault(turn * units + unit, []).append(events[at][0])
                    at += 1
                clock = start + unit_us
        after = [event for event, _ in events[at:]]
        plans.append((pieces, before_unit, after))
    return parts, plans


def gather_product_kernel(
    rows, parts, plans, size,
    place_ref, choice_ref, own_ref, a_ref, all_ref, mine_ref, other_ref,
    staged, mixed, spare, a_stage, b_high, b_low, acc, mine,
    send_sem, recv_sem, load_sem, keep_sem, a_sem, mine_sem, swap_send, swap_recv,
    lend_send, lend_recv, spare_sem,
):
    here = lax.axis_index("row")
    sibling = 1 - lax.axis_index("col")
    lines = rows // 2
    z, y = here // 2, here % 2
    count = parts[-1][1]
    chunk_rows = a_stage.shape[2]
    chunks = a_ref.shape[1] // chunk_rows
    width = b_high.shape[1]
    blocks = width // size
    beside = z * 2 + (1 - y)
    up, down = here + 2, here - 2
    has_up, has_down = z < lines - 1, z > 0

    most = own_ref.shape[0] - SPARE
    mixed_at = parts[3][0]

    def copy(part, origin, way, target, own=False):
        low, high = parts[part]
        span = pl.ds(low, high - low)
        source = mixed if part == 3 else own_ref.at[span]
        return pltpu.make_async_remote_copy(
            src_ref=source if own else all_ref.at[origin, span],
            dst_ref=all_ref.at[origin, span],
            send_sem=send_sem.at[part, origin, way],
            recv_sem=recv_sem.at[part, origin],
            device_id={"row": target},
            device_id_type=pl.DeviceIdType.MESH,
        )

    def lend(origin):
        return pltpu.make_async_remote_copy(
            src_ref=all_ref.at[origin, pl.ds(count - SPARE, SPARE)],
            dst_ref=all_ref.at[origin, pl.ds(most, SPARE)],
            send_sem=lend_send.at[origin],
            recv_sem=lend_recv.at[origin],
            device_id={"col": sibling},
            device_id_type=pl.DeviceIdType.MESH,
        )

    def arrived(part, origin):
        copy(part, origin, 0, beside).wait_recv()

    barrier = pltpu.get_barrier_semaphore()

    def greet(target):
        pl.semaphore_signal(barrier, inc=1, device_id=target, device_id_type=pl.DeviceIdType.MESH)

    greet({"row": beside})
    greet({"col": sibling})

    @pl.when(has_up)
    def _():
        greet({"row": up})

    @pl.when(has_down)
    def _():
        greet({"row": down})

    pl.semaphore_wait(barrier, 2 + has_up.astype(jnp.int32) + has_down.astype(jnp.int32))

    spare_copy = pltpu.make_async_remote_copy(
        src_ref=own_ref.at[pl.ds(count, SPARE)],
        dst_ref=spare,
        send_sem=spare_sem.at[0],
        recv_sem=spare_sem.at[1],
        device_id={"col": sibling},
        device_id_type=pl.DeviceIdType.MESH,
    )
    spare_copy.start()
    mixed_copy = pltpu.make_async_copy(
        own_ref.at[pl.ds(mixed_at, count - mixed_at)], mixed, keep_sem
    )
    mixed_copy.start()

    def send_own(part):
        @pl.when(has_up)
        def _():
            copy(part, here, 0, up, True).start()

        @pl.when(has_down)
        def _():
            copy(part, here, 1, down, True).start()

        if part:
            copy(part, here, 2, beside, True).start()

    copy(0, here, 2, beside, True).start()
    send_own(1)
    send_own(2)
    own_loads = [
        pltpu.make_async_copy(own_ref.at[pl.ds(0, count)], staged.at[pl.ds(1, count)], load_sem.at[0])
    ] + [
        pltpu.make_async_copy(
            own_ref.at[count + at], staged.at[count + SPARE - at], load_sem.at[1 + at]
        )
        for at in range(SPARE)
    ]
    for load in own_loads:
        load.start()
    mixed_copy.wait()
    spare_copy.wait()
    for at in range(SPARE):
        target = count - SPARE + at - mixed_at
        mixed[target] = jnp.where(choice_ref[1 + at] > 0, mixed[target], spare[SPARE - 1 - at])
    for load in own_loads:
        load.wait()
    send_own(3)
    send_own(0)

    def origin_of(turn):
        origin = here
        for line, (pieces, _, _) in enumerate(plans):
            for at, (from_line, side) in enumerate(pieces):
                origin = jnp.where(
                    (z == line) & (turn == at), from_line * 2 + (y if side == 0 else 1 - y), origin
                )
        return origin

    def a_copy(step, origin):
        chunk = step % chunks
        return pltpu.make_async_copy(
            a_ref.at[
                :,
                pl.ds(pl.multiple_of(chunk * chunk_rows, 8), chunk_rows),
                pl.ds(pl.multiple_of(origin * width, 128), width),
            ],
            a_stage.at[step % 2],
            a_sem.at[step % 2],
        )

    a_copy(0, origin_of(0)).start()
    a_copy(1, origin_of(1 // chunks)).start()
    acc[...] = jnp.zeros_like(acc)
    staged[0] = jnp.zeros(staged.shape[1:], F32)

    def relay(line, item):
        from_line, side, part = item
        origin = from_line * 2 + (y if side == 0 else 1 - y)
        arrived(part, origin)
        if part == 3:
            lend(origin).start()
        if side == 1 and part:
            return
        if from_line == line:
            ways = ([0] if line < lines - 1 else []) + ([1] if line > 0 else [])
        elif from_line < line:
            ways = [0] if line < lines - 1 else []
        else:
            ways = [1] if line > 0 else []
        for way in ways:
            copy(part, origin, way, up if way == 0 else down).start()
        if side == 0 and part:
            copy(part, origin, 2, beside).start()

    def a_step(step, _):
        turn, chunk = step // chunks, step % chunks
        for line, (pieces, before_unit, _) in enumerate(plans):
            @pl.when(z == line)
            def _():
                for at in sorted(before_unit):
                    @pl.when(step == at)
                    def _():
                        for item in before_unit[at]:
                            relay(line, item)

        @pl.when(chunk == 0)
        def _():
            for line, (pieces, _, _) in enumerate(plans):
                for at, (from_line, side) in enumerate(pieces):
                    if side == 1:
                        @pl.when((z == line) & (turn == at))
                        def _():
                            for part in (1, 2):
                                arrived(part, from_line * 2 + (1 - y))

            origin = origin_of(turn)

            def keeps():
                return [
                    pltpu.make_async_copy(
                        staged.at[pl.ds(1, count)], all_ref.at[here, pl.ds(0, count)], keep_sem
                    ),
                    pltpu.make_async_copy(
                        staged.at[pl.ds(1 + count, SPARE)], all_ref.at[here, pl.ds(most, SPARE)],
                        load_sem.at[1],
                    ),
                ]

            @pl.when(turn == 0)
            def _():
                for keep in keeps():
                    keep.start()

            @pl.when(turn == 1)
            def _():
                for keep in keeps():
                    keep.wait()

            @pl.when(turn > 0)
            def _():
                load = pltpu.make_async_copy(
                    all_ref.at[origin, pl.ds(0, count)], staged.at[pl.ds(1, count)], load_sem.at[0]
                )
                load.start()
                lend(origin).wait_recv()
                lent = pltpu.make_async_copy(
                    all_ref.at[origin, pl.ds(most, SPARE)], staged.at[pl.ds(1 + count, SPARE)],
                    load_sem.at[1],
                )
                lent.start()
                load.wait()
                lent.wait()

            def spread(block, _):
                span = pl.ds(pl.multiple_of(block * size, size), size)
                for slot in range(4):
                    value = staged[place_ref[origin * (4 * blocks) + slot * blocks + block]]
                    for kind, term in enumerate((value[0], value[1], value[0] + value[1])):
                        high, low = halves(term)
                        b_high[kind, span, slot * size:(slot + 1) * size] = high
                        b_low[kind, span, slot * size:(slot + 1) * size] = low
                return 0

            lax.fori_loop(0, blocks, spread, 0)

        a_copy(step, here).wait()
        span = pl.ds(pl.multiple_of(chunk * chunk_rows, 8), chunk_rows)
        real, imag = a_stage[step % 2, 0], a_stage[step % 2, 1]
        for kind, term in enumerate((real, imag, real + imag)):
            high, low = halves(term)
            acc[kind, span, :] += jnp.dot(
                jnp.concatenate([high, low, high], axis=1),
                jnp.concatenate([b_high[kind], b_high[kind], b_low[kind]], axis=0),
                preferred_element_type=F32,
            )

        @pl.when(step + 2 < rows * chunks)
        def _():
            a_copy(step + 2, origin_of((step + 2) // chunks)).start()

        @pl.when(turn == rows - 1)
        def _():
            for slot in range(4):
                columns = slice(slot * size, (slot + 1) * size)
                first, second = acc[0, span, columns], acc[1, span, columns]
                mine[slot, 0, span] = first - second
                mine[slot, 1, span] = acc[2, span, columns] - first - second
            swap(chunk).start()
            keep_mine(chunk).start()

        return 0

    def swap(chunk):
        span = pl.ds(pl.multiple_of(chunk * chunk_rows, 8), chunk_rows)
        return pltpu.make_async_remote_copy(
            src_ref=mine.at[:, :, span],
            dst_ref=other_ref.at[:, :, span],
            send_sem=swap_send.at[chunk],
            recv_sem=swap_recv.at[chunk],
            device_id={"col": sibling},
            device_id_type=pl.DeviceIdType.MESH,
        )

    def keep_mine(chunk):
        span = pl.ds(pl.multiple_of(chunk * chunk_rows, 8), chunk_rows)
        return pltpu.make_async_copy(mine.at[:, :, span], mine_ref.at[:, :, span], mine_sem.at[chunk])

    lax.fori_loop(0, rows * chunks, a_step, 0)

    for line, (_, _, after) in enumerate(plans):
        if after:
            @pl.when(z == line)
            def _():
                for item in after:
                    relay(line, item)

    for chunk in range(chunks):
        swap(chunk).wait()
        keep_mine(chunk).wait()

    copy(0, here, 2, beside, True).wait_send()
    for line in range(lines):
        lend(line * 2 + (1 - y)).wait_send()

        @pl.when(z != line)
        def _():
            lend(line * 2 + y).wait_send()

        for part in (1, 2, 3):
            copy(part, line * 2 + y, 2, beside).wait_send()
        for part, origin in [(part, line * 2 + y) for part in (1, 2, 3, 0)] + [(0, line * 2 + 1 - y)]:
            @pl.when(has_up & (line <= z))
            def _():
                copy(part, origin, 0, up).wait_send()

            @pl.when(has_down & (line >= z))
            def _():
                copy(part, origin, 1, down).wait_send()


def gather_product(packed, place, choice, ancestor_inverse, count, branch, size):
    rows = lax.axis_size("row")
    tile_rows, half_rows = ancestor_inverse.shape[1:]
    width = half_rows // rows
    chunk_rows = math.gcd(tile_rows, ROW_CHUNK)
    chunks = tile_rows // chunk_rows
    parts, plans = relay_plan(rows // 2, count, 2.82, 16.0 / chunks, chunks)
    column_shape = jax.ShapeDtypeStruct((4, 2, tile_rows, size), F32)
    return pl.pallas_call(
        functools.partial(gather_product_kernel, rows, parts, plans, size),
        out_shape=(
            jax.ShapeDtypeStruct((rows,) + packed.shape, F32), column_shape, column_shape,
        ),
        in_specs=[
            pl.BlockSpec(memory_space=pltpu.SMEM),
            pl.BlockSpec(memory_space=pltpu.SMEM),
            pl.BlockSpec(memory_space=pl.ANY),
            pl.BlockSpec(memory_space=pl.ANY),
        ],
        out_specs=(pl.BlockSpec(memory_space=pl.ANY),) * 3,
        scratch_shapes=[
            pltpu.VMEM((count + 1 + SPARE,) + packed.shape[1:], F32),
            pltpu.VMEM((count - parts[3][0],) + packed.shape[1:], F32),
            pltpu.VMEM((SPARE,) + packed.shape[1:], F32),
            pltpu.VMEM((2, 2, chunk_rows, width), F32),
            pltpu.VMEM((3, width, 4 * size), BF16),
            pltpu.VMEM((3, width, 4 * size), BF16),
            pltpu.VMEM((3, tile_rows, 4 * size), F32),
            pltpu.VMEM((4, 2, tile_rows, size), F32),
            pltpu.SemaphoreType.DMA((4, rows, 3)),
            pltpu.SemaphoreType.DMA((4, rows)),
            pltpu.SemaphoreType.DMA((1 + SPARE,)),
            pltpu.SemaphoreType.DMA,
            pltpu.SemaphoreType.DMA((2,)),
            pltpu.SemaphoreType.DMA((chunks,)),
            pltpu.SemaphoreType.DMA((chunks,)),
            pltpu.SemaphoreType.DMA((chunks,)),
            pltpu.SemaphoreType.DMA((rows,)),
            pltpu.SemaphoreType.DMA((rows,)),
            pltpu.SemaphoreType.DMA((2,)),
        ],
        compiler_params=pltpu.CompilerParams(
            collective_id=branch + 1, has_side_effects=True, vmem_limit_bytes=VMEM_BYTES
        ),
    )(place, choice, packed, ancestor_inverse)


def wide(matrix):
    return jnp.concatenate([matrix[0], matrix[1]], axis=1)


def folded(product, size):
    return jnp.stack(
        [
            product[:size, :size] - product[size:, size:],
            product[:size, size:] + product[size:, :size],
        ]
    )


def contracted(left_side, right_side):
    return lax.dot_general(
        left_side, right_side, (((0,), (0,)), ((), ())), preferred_element_type=F32
    )


def tripled(value, axis, right):
    high, low = halves(value)
    return jnp.concatenate([high, high, low] if right else [high, low, high], axis=axis)


def finish_kernel(
    size, live_ref, order_ref, window_at_ref,
    mine_ref, other_ref, link_ref, w0_ref, w1_ref, w2_ref, w3_ref,
    columns_ref, sums_ref, acc,
):
    row = pl.program_id(0)
    windows = (w0_ref, w1_ref, w2_ref, w3_ref)

    @pl.when(row == 0)
    def _():
        acc[...] = jnp.zeros_like(acc)

    for tree in range(2):
        child = tree + 2
        parent_at = order_ref[tree]
        child_at = order_ref[child]

        @pl.when(live_ref[tree, row] == 0)
        def _():
            columns_ref[parent_at] = jnp.zeros(columns_ref.shape[1:], F32)

        @pl.when(live_ref[child, row] == 0)
        def _():
            columns_ref[child_at] = jnp.zeros(columns_ref.shape[1:], F32)

        @pl.when(live_ref[tree, row] > 0)
        def _():
            columns_ref[parent_at] = -(mine_ref[tree] + other_ref[tree])

        @pl.when(live_ref[child, row] > 0)
        def _():
            parent = columns_ref[parent_at]
            linked = jnp.dot(
                tripled(jnp.concatenate([parent[0], parent[1]], axis=0), 1, False),
                tripled(wide(link_ref[tree]), 0, True),
                preferred_element_type=F32,
            )
            columns_ref[child_at] = -(mine_ref[child] + other_ref[child] + folded(linked, size))

        @pl.when((live_ref[4, row] > 0) & (live_ref[tree, row] > 0))
        def _():
            parent = tripled(wide(columns_ref[parent_at]), 0, True)

            @pl.when(live_ref[child, row] == 0)
            def _():
                acc[tree, :2 * size, :2 * size] += contracted(
                    tripled(wide(windows[tree][0]), 0, False), parent
                )

            @pl.when(live_ref[child, row] > 0)
            def _():
                acc[tree] += contracted(
                    jnp.concatenate(
                        [tripled(wide(windows[at][0]), 0, False) for at in (tree, child)], axis=1
                    ),
                    jnp.concatenate(
                        [parent, tripled(wide(columns_ref[child_at]), 0, True)], axis=1
                    ),
                )

    @pl.when(row == pl.num_programs(0) - 1)
    def _():
        for tree in range(2):
            for kind, (high, wide_at) in enumerate(((0, 0), (1, 0), (1, 1))):
                block = acc[
                    tree, 2 * size * high:2 * size * (high + 1),
                    2 * size * wide_at:2 * size * (wide_at + 1),
                ]
                sums_ref[2 * kind + tree] = folded(block, size)


def finish(mine, other, coupling, gathered, live, tree_order, window_at, size):
    rows = live.shape[1]
    gathered = gathered.reshape((-1,) + gathered.shape[2:])

    def window_map(slot, g, live, order, window_at):
        return (window_at[slot, g], 0, 0, 0)

    return pl.pallas_call(
        functools.partial(finish_kernel, size),
        out_shape=(
            jax.ShapeDtypeStruct(mine.shape, F32),
            jax.ShapeDtypeStruct((6, 2, size, size), F32),
        ),
        grid_spec=pltpu.PrefetchScalarGridSpec(
            num_scalar_prefetch=3,
            grid=(rows,),
            in_specs=[
                pl.BlockSpec((4, 2, size, size), lambda g, *_: (0, 0, g, 0)),
                pl.BlockSpec((4, 2, size, size), lambda g, *_: (0, 0, g, 0)),
                pl.BlockSpec(coupling.shape, lambda g, *_: (0, 0, 0, 0)),
            ]
            + [
                pl.BlockSpec((1, 2, size, size), functools.partial(window_map, slot))
                for slot in range(4)
            ],
            out_specs=(
                pl.BlockSpec((4, 2, size, size), lambda g, *_: (0, 0, g, 0)),
                pl.BlockSpec((6, 2, size, size), lambda g, *_: (0, 0, 0, 0)),
            ),
            scratch_shapes=[pltpu.VMEM((2, 4 * size, 4 * size), F32)],
        ),
        compiler_params=pltpu.CompilerParams(vmem_limit_bytes=VMEM_BYTES),
    )(live, tree_order, window_at, mine, other, coupling, gathered, gathered, gathered, gathered)


def close_kernel(size, order_ref, totals_ref, diag_ref, link_ref, diagonal_ref, cross_ref):
    def times(left_side, right_side):
        return folded(
            matmul(jnp.concatenate([left_side[0], left_side[1]], axis=0), wide(right_side)), size
        )

    for tree in range(2):
        parent_at, child_at = order_ref[tree], order_ref[tree + 2]
        link = link_ref[tree]
        parent = diag_ref[parent_at] - totals_ref[tree]
        crossed = jnp.stack([totals_ref[2 + tree, part].T for part in range(2)])
        cross = -(crossed + times(parent, link))
        turned = jnp.stack([link[part].T for part in range(2)])
        diagonal_ref[parent_at] = parent
        cross_ref[tree] = cross
        diagonal_ref[child_at] = diag_ref[child_at] - totals_ref[4 + tree] - times(turned, cross)


def close(totals, diag_inverse, coupling, tree_order, size):
    whole = pl.BlockSpec(memory_space=pltpu.VMEM)
    return pl.pallas_call(
        functools.partial(close_kernel, size),
        out_shape=(
            jax.ShapeDtypeStruct(diag_inverse.shape, F32),
            jax.ShapeDtypeStruct(coupling.shape, F32),
        ),
        in_specs=[pl.BlockSpec(memory_space=pltpu.SMEM), whole, whole, whole],
        out_specs=(whole, whole),
    )(tree_order, totals, diag_inverse, coupling)


def sum_kernel(routes, part_ref, sum_ref, total, landed, send_sem, recv_sem):
    barrier = pltpu.get_barrier_semaphore()

    def place_of(stage):
        axis, bits = stage
        at = lax.axis_index(axis)
        return at, [(at // (1 << bit)) % 2 for bit in bits]

    def peers(stage):
        at, values = place_of(stage)
        found = []
        for mask in range(1, 1 << len(values)):
            target, index = at, 0
            for spot, (bit, value) in enumerate(zip(stage[1], values)):
                turned = mask >> spot & 1
                target = target + turned * (1 << bit) * (1 - 2 * value)
                index = index + (1 << spot) * ((1 - value) if turned else value)
            found.append((mask, target, index))
        return found

    greeted = [(stage[0], target) for stage in routes[0] for _, target, _ in peers(stage)]
    for axis, target in greeted:
        pl.semaphore_signal(
            barrier, inc=1, device_id={axis: target}, device_id_type=pl.DeviceIdType.MESH
        )
    pl.semaphore_wait(barrier, len(greeted))

    def copy(route, turn, mask, axis, target, source, source_at, sink, sink_at, length):
        return pltpu.make_async_remote_copy(
            src_ref=source.at[pl.ds(source_at, length)],
            dst_ref=sink.at[pl.ds(sink_at, length)],
            send_sem=send_sem.at[route, turn, mask],
            recv_sem=recv_sem.at[route, turn, mask],
            device_id={axis: target},
            device_id_type=pl.DeviceIdType.MESH,
        )

    total[...] = part_ref[...]
    stages = len(routes[0])
    whole = part_ref.shape[0] // len(routes)
    starts = [whole * route for route in range(len(routes))]
    lengths = [whole] * len(routes)
    landings = list(starts)
    spans = [[] for _ in routes]
    for turn in range(stages):
        moves = [[] for _ in routes]
        for route, order in enumerate(routes):
            stage = order[turn]
            lengths[route] //= 1 << len(stage[1])
            for mask, target, index in peers(stage):
                give = pl.multiple_of(starts[route] + index * lengths[route], 8)
                landing = landings[route]
                move = copy(
                    route, turn, mask, stage[0], target, total, give, landed, landing, lengths[route]
                )
                move.start()
                moves[route].append((move, landing))
                landings[route] = landing + lengths[route]
        for route, order in enumerate(routes):
            index = 0
            for spot, value in enumerate(place_of(order[turn])[1]):
                index = index + (1 << spot) * value
            keep = pl.multiple_of(starts[route] + index * lengths[route], 8)
            for move, landing in moves[route]:
                move.wait()
                total[pl.ds(keep, lengths[route])] += landed[pl.ds(landing, lengths[route])]
            starts[route] = keep
            spans[route].append((keep, lengths[route]))
    for route in range(len(routes)):
        span = pl.ds(starts[route], lengths[route])
        sum_ref[span] = total[span]
    for turn in reversed(range(stages)):
        moves = []
        for route, order in enumerate(routes):
            keep, length = spans[route][turn]
            for mask, target, _ in peers(order[turn]):
                move = copy(
                    route, stages + turn, mask, order[turn][0], target,
                    sum_ref, keep, sum_ref, keep, length,
                )
                move.start()
                moves.append(move)
        for move in moves:
            move.wait()


def summed(parts):
    counts = [lax.axis_size(axis) for axis in ("col", "row")]
    if any(count & (count - 1) or count < 2 for count in counts):
        return lax.psum(parts, ("row", "col"))
    bits = [count.bit_length() - 1 for count in counts]
    line_bits = tuple(range(1, bits[1]))
    stages = [("col", (bit,)) for bit in range(bits[0])] + [("row", (0,))]
    stages += [("row", line_bits[at:at + 2]) for at in range(0, len(line_bits), 2)]
    flat = parts.reshape(-1, parts.shape[-1])
    if flat.shape[0] % (16 << sum(bits)) or len(stages) < 3:
        return lax.psum(parts, ("row", "col"))
    routes = (tuple(stages), (*stages[:bits[0]], *stages[bits[0] + 1:], stages[bits[0]]))
    total = pl.pallas_call(
        functools.partial(sum_kernel, routes),
        out_shape=jax.ShapeDtypeStruct(flat.shape, F32),
        in_specs=[pl.BlockSpec(memory_space=pltpu.VMEM)],
        out_specs=pl.BlockSpec(memory_space=pltpu.VMEM),
        scratch_shapes=[
            pltpu.VMEM(flat.shape, F32),
            pltpu.VMEM(flat.shape, F32),
            pltpu.SemaphoreType.DMA((2, 2 * len(stages), 4)),
            pltpu.SemaphoreType.DMA((2, 2 * len(stages), 4)),
        ],
        compiler_params=pltpu.CompilerParams(collective_id=0, has_side_effects=True),
    )(flat)
    return total.reshape(parts.shape)


def per_device_blocks(
    ancestor_inverse, factor_panels, diag_inverse, coupling, block_pattern, tree_order
):
    size = factor_panels.shape[3]
    most = 4 * (factor_panels.shape[2] // size)
    least = (most + 1) // 2
    sizes = sorted({*range(least + 2, min(least + 7, most)), least + (most - least) * 2 // 3, most})
    sizes = [size_of for size_of in sizes if size_of - part_cuts(size_of)[3] >= SPARE]
    place, window_at, live, choice, packed = prepare(
        block_pattern, tree_order, factor_panels, sizes
    )

    def branch(at):
        return lambda blocks: gather_product(
            blocks, place, choice, ancestor_inverse, sizes[at], at, size
        )

    gathered, mine, other = lax.switch(choice[0], [branch(at) for at in range(len(sizes))], packed)
    inverse_panels, sums = finish(
        mine, other, coupling, gathered, live, tree_order, window_at, size
    )
    inverse_diagonal, crosses = close(summed(sums), diag_inverse, coupling, tree_order, size)
    return (inverse_panels, inverse_diagonal, crosses)


def per_device(ancestor_inverse, factor_panels, diag_inverse, coupling, block_pattern, tree_order):
    size = factor_panels.shape[3]
    rows = lax.axis_size("row")
    whole_blocks = math.gcd(ancestor_inverse.shape[1], factor_panels.shape[2]) % size == 0
    paired = rows % 2 == 0 and rows >= 4 and lax.axis_size("col") == 2
    blocks = whole_blocks and size % 128 == 0 and paired and ancestor_inverse.shape[1] <= 1536
    run = per_device_blocks if blocks else per_device_dense
    return run(ancestor_inverse, factor_panels, diag_inverse, coupling, block_pattern, tree_order)


def solution(mesh):
    return jax.shard_map(
        per_device,
        mesh=mesh,
        in_specs=(
            P(None, ("pole", "row"), "col"),
            P(None, None, ("pole", "col", "row"), None),
            P("pole", None, None, None),
            P("pole", None, None, None),
            P(),
            P(),
        ),
        out_specs=(
            P(None, None, ("pole", "row"), None),
            P("pole", None, None, None),
            P("pole", None, None, None),
        ),
        check_vma=False,
    )
```
